32 devices in a mesh: lat: 4 (over y, x), lon: 8 (over z, core).
Axes of the slice: x: 2, y: 2, z: 4, core: 2. Of those that a mesh axis runs over, the one named last changes fastest.
Arguments:
- wind_u: float32 [32, 32, 1024], P(None, 'lat', 'lon'), may hold values from -6 to 6
- wind_v: float32 [32, 32, 1024], P(None, 'lat', 'lon'), may hold values from -6 to 6
Outputs:
- modes: float32 [32, 2, 32, 1024], P(None, None, 'lat', 'lon')
- factor: float32 [32, 32], replicated
The draws below stay inside these ranges and needn't reach their ends.
All inputs are finite; a program needn't handle non-finite values.
Results may differ from the reference program's by a relative error of at most 0.0003.
Values sent between devices are 32-bit elements; how exact they have to be, the bound alone decides.
A program may use at most 64 MiB of HBM per device.

```python
import math
import jax
import jax.numpy as jnp
from jax import lax

SNAPS = 32
NLAT = 32
NLON = 1024
ROWS = 65536


def wind_field(key, offset):
    keys = [jax.random.fold_in(key, offset + number) for number in range(4)]
    lat_frac = jnp.arange(NLAT).astype(jnp.float32) / NLAT
    lon_frac = jnp.arange(NLON).astype(jnp.float32) / NLON
    noise = jax.random.normal(keys[0], (SNAPS, NLAT, NLON), jnp.float32)
    ramp = 3.0 ** (0.5 * lat_frac[:, None] + 0.5 * lon_frac[None, :])
    base = jax.random.uniform(keys[1], (NLAT, NLON), jnp.float32, -1.2, 1.2)
    cells = jnp.exp(jax.random.uniform(keys[2], (NLAT, NLON), jnp.float32, 0.0, math.log(3.4)))
    raw_snaps = jnp.exp(jax.random.uniform(keys[3], (SNAPS, 1, 1), jnp.float32, 0.0, math.log(10.0)))
    snaps = raw_snaps / jnp.min(raw_snaps)
    field = 0.025 * snaps * (ramp * cells)[None, :, :] * (base[None, :, :] + noise / 30.0)
    return jnp.clip(field, -6.0, 6.0)


def draw_wind_u(key, part):
    return wind_field(key, 100)


def draw_wind_v(key, part):
    return wind_field(key, 200)


def setup_inputs(seed: int = 0) -> dict:
    seeds = jax.random.split(jax.random.key(seed), 3)
    wind_u = draw_wind_u(jax.random.fold_in(seeds[2], 71), 0)
    wind_v = draw_wind_v(jax.random.fold_in(seeds[2], 71), 0)
    return {"wind_u": wind_u, "wind_v": wind_v}


def upper_factor(gram):
    count = gram.shape[0]
    positions = jnp.arange(count)

    def column_step(k, state):
        rest, lower = state
        onehot = (positions == k).astype(jnp.float32)
        below = (positions >= k).astype(jnp.float32)
        pivot = jnp.sum(rest * onehot[:, None] * onehot[None, :])
        column = lax.optimization_barrier(jnp.sum(rest * onehot[None, :], axis=1)) * below / jnp.sqrt(pivot)
        lower = lower + column[:, None] * onehot[None, :]
        rest = rest - column[:, None] * column[None, :]
        return (rest, lower)
    start = (gram.astype(jnp.float32), jnp.zeros(gram.shape, jnp.float32))
    rest, lower = lax.fori_loop(0, count, column_step, start)
    return lower.T

def inverse_upper(upper):
    count = upper.shape[0]
    positions = jnp.arange(count)

    def row_step(i, result):
        k = count - 1 - i
        onehot = (positions == k).astype(jnp.float32)
        row_of = lax.optimization_barrier(jnp.sum(upper * onehot[:, None], axis=0))
        diag = jnp.sum(row_of * onehot)
        off_diag = row_of * (1.0 - onehot)
        new_row = (onehot - lax.optimization_barrier(jnp.sum(off_diag[:, None] * result, axis=0))) / diag
        return result + onehot[:, None] * new_row[None, :]
    return lax.fori_loop(0, count, row_step, jnp.zeros(upper.shape, jnp.float32))

def build_columns(wind_u, wind_v):
    step = 2.0 * math.pi / NLON
    index = jnp.arange(NLAT).astype(jnp.float32)
    cosines = jnp.cos((index + 0.5 - NLAT / 2) * step)
    weight_c = cosines[None, :, None]

    def lat_diff(field):
        padded = jnp.pad(field * weight_c, ((0, 0), (1, 1), (0, 0)))
        return padded[:, 2:, :] - padded[:, :-2, :]

    def lon_diff(field):
        return jnp.roll(field, -1, axis=2) - jnp.roll(field, 1, axis=2)
    scale = (0.5 / jnp.sqrt(cosines))[None, :, None]
    vorticity = (lon_diff(wind_v) - lat_diff(wind_u)) * scale
    divergence = (lon_diff(wind_u) + lat_diff(wind_v)) * scale
    return jnp.stack([vorticity, divergence], axis=1)

def reference(wind_u, wind_v):
    highest = lax.Precision.HIGHEST
    block = build_columns(wind_u, wind_v).reshape(SNAPS, -1)
    gram_one = jnp.dot(block, block.T, precision=highest, preferred_element_type=jnp.float32)
    first = upper_factor(gram_one)
    solved = jnp.dot(inverse_upper(first).T, block, precision=highest, preferred_element_type=jnp.float32)
    gram_two = jnp.dot(solved, solved.T, precision=highest, preferred_element_type=jnp.float32)
    second = upper_factor(gram_two)
    root = math.sqrt(ROWS)
    modes = jnp.dot(inverse_upper(second).T, solved, precision=highest, preferred_element_type=jnp.float32) * root
    factor = jnp.dot(second, first, precision=highest, preferred_element_type=jnp.float32) / root
    return (modes.reshape(SNAPS, 2, NLAT, NLON), factor)
```

```python
import functools
import math

import jax
import jax.numpy as jnp
from jax import lax
from jax.experimental import pallas as pl
from jax.experimental.pallas import tpu as pltpu
from jax.sharding import PartitionSpec as P

MESH = pl.DeviceIdType.MESH
LANES = 128
SUBS = 8
BLOCK = 8
VMEM_BYTES = 8 * 1024 * 1024


def iota(shape, dim):
    return lax.broadcasted_iota(jnp.int32, shape, dim)


def dot(left, right, dims):
    return lax.dot_general(
        left,
        right,
        (dims, ((), ())),
        precision=lax.Precision.HIGHEST,
        preferred_element_type=jnp.float32,
    )


def two(tile):
    high = tile.astype(jnp.bfloat16)
    return high, (tile - high.astype(jnp.float32)).astype(jnp.bfloat16)


def pair_dot(left, right, dims):
    a, b = two(left)
    x, y = two(right)

    def one(m, n):
        return lax.dot_general(m, n, (dims, ((), ())), preferred_element_type=jnp.float32)

    return one(a, x) + (one(a, y) + one(b, x))


def roll(tile, shift):
    shift = shift % LANES
    return tile if shift == 0 else pltpu.roll(tile, shift, 1)


def spread(tile):
    return jnp.broadcast_to(tile, (SUBS, LANES))


def two_sum(a, b):
    total = a + b
    part = total - a
    return total, (a - (total - part)) + (b - part)


def power_above(bound):
    wide = bound * (2.0**23 + 1.0)
    return 2.0 * jnp.abs(wide - wide * (1.0 - 2.0**-24))


def fixed_slices(tile, unit, bits):
    out = []
    for count in bits:
        magic = unit * (1.5 * 2.0 ** (23 - count))
        part = (tile + magic) - magic
        out.append(part.astype(jnp.bfloat16))
        tile = tile - part
    out.append(tile.astype(jnp.bfloat16))
    return out


def factorize(rows, n):
    groups = n // SUBS
    lane = iota((SUBS, LANES), 1)
    sub = iota((SUBS, LANES), 0)
    rows = list(rows)
    pivots = [None] * groups
    lower = [jnp.zeros((SUBS, LANES), jnp.float32)] * groups
    across = jnp.ones((SUBS, LANES), jnp.float32)
    for start in range(0, n, BLOCK):
        r = start // SUBS
        columns = [
            [spread(rows[g][:, n + k : n + k + 1]) if g >= r else None for g in range(groups)]
            for k in range(start, start + BLOCK)
        ]
        for step in range(BLOCK):
            k = start + step
            s = k % SUBS
            pivot = spread(columns[step][r][s : s + 1, :])
            pivots[r] = pivot if s == 0 else jnp.where(sub == s, pivot, pivots[r])
            across = jnp.where(lane == n + k, pivot, across)
            inverse = 1.0 / pivot
            pivot_row = spread(rows[r][s : s + 1, :]) * inverse
            heads = [
                spread(columns[later][r][s : s + 1, :]) * inverse for later in range(step + 1, BLOCK)
            ]
            for g in range(r, groups):
                factor = columns[step][g]
                lower[g] = jnp.where(lane == n + k, factor, lower[g])
                if g == r:
                    if s == SUBS - 1:
                        continue
                    factor = jnp.where(sub > s, factor, 0.0)
                rows[g] = rows[g] - factor * pivot_row
                for later in range(step + 1, BLOCK):
                    columns[later][g] = columns[later][g] - factor * heads[later - step - 1]
    across = 1.0 / jnp.sqrt(across)
    out, left = [], []
    for g in range(groups):
        scaled = rows[g] * (1.0 / jnp.sqrt(pivots[g]))
        at = lane - n - g * SUBS
        out.append(jnp.where((lane < n) | (at >= sub), scaled, 0.0))
        left.append(jnp.where((lane >= n) & (at <= sub), lower[g] * across, 0.0))
    return jnp.concatenate(out, axis=0), jnp.concatenate(left, axis=0)


def packed_gram(block, n):
    groups = n // SUBS
    peak = jnp.max(jnp.abs(block), axis=1, keepdims=True)
    unit = power_above(jnp.broadcast_to(peak, (n, LANES)))
    pieces = []
    for at in range(0, block.shape[1], LANES):
        pieces.append(fixed_slices(block[:, at : at + LANES], unit, (5, 12, 19)))
    stack = jnp.concatenate(
        [jnp.concatenate([piece[a] for piece in pieces], axis=1) for a in range(4)], axis=0
    )
    gram = lax.dot_general(
        stack, stack, (((1,), (1,)), ((), ())), preferred_element_type=jnp.float32
    )
    quarter = iota((SUBS, LANES), 1) // n

    def tile(a, g):
        at = a * n + g * SUBS
        return roll(gram[at : at + SUBS], a * n)

    near, far = [], []
    for g in range(groups):
        turned = [tile(a, g) for a in range(4)]
        held = [turned[0]] + [jnp.where(quarter >= a, turned[a], 0.0) for a in range(1, 4)]
        past = [jnp.where(quarter < a, turned[a], 0.0) for a in range(1, 4)]
        near.append((held[0] + held[3]) + (held[1] + held[2]))
        far.append((past[0] + past[2]) + past[1])

    def gather(tiles, order):
        total = None
        for g in range(groups):
            moved = roll(tiles[g], n * (g - order))
            total = moved if total is None else jnp.where(quarter == g, moved, total)
        return total

    order = [gather(near, o) for o in range(4)]
    rest = gather(far, 0) + (gather(far, 1) + gather(far, 2))
    high, low = two_sum(order[0], order[1])
    high, more = two_sum(high, order[2])
    return two_sum(high, (low + more) + (order[3] + rest))


def residual(high, low, lower, n):
    groups = n // SUBS
    lane = iota((SUBS, LANES), 1)
    sub = iota((SUBS, LANES), 0)
    unpacked = [roll(high, -g * n) for g in range(groups)]
    diagonal = jnp.concatenate(
        [jnp.where(lane == sub + g * SUBS, unpacked[g], 0.0) for g in range(groups)], axis=0
    )
    peak = jnp.sqrt(jnp.sum(diagonal, axis=1, keepdims=True)) * 1.01
    unit = power_above(jnp.broadcast_to(peak, (n, LANES)))
    slices = fixed_slices(lower, unit, (8, 17, 26))
    stack = jnp.concatenate(slices, axis=0)
    products = [
        lax.dot_general(
            stack[:, : 2 * n],
            one[:, : 2 * n],
            (((1,), (1,)), ((), ())),
            preferred_element_type=jnp.float32,
        )
        for one in slices
    ]

    def order(count):
        total = None
        for a in range(4):
            b = count - a
            if 0 <= b < 4:
                one = products[b][a * n : (a + 1) * n]
                total = one if total is None else total + one
        return total

    def rows_of(packed):
        return jnp.concatenate(
            [roll(packed, -g * n)[:, :n] for g in range(groups)], axis=0
        )

    first, low_one = two_sum(rows_of(high), -order(0))
    first, low_two = two_sum(first, -order(1))
    first, low_three = two_sum(first, -order(2))
    tail = (low_one + low_two) + (low_three + (rows_of(low) - (order(3) + (order(4) + order(5)))))
    return first + tail


def kernel(
    sizes,
    root,
    u_hbm,
    v_hbm,
    modes_ref,
    factor_ref,
    wind_ref,
    x_ref,
    lat_out,
    lat_in,
    lon_out,
    lon_in,
    pair_buf,
    chip_buf,
    lat_send,
    lat_recv,
    lon_send,
    lon_recv,
    pair_send,
    pair_recv,
    chip_send,
    chip_recv,
    relay_sem,
    local_sem,
):
    lat_size, lon_size, cores = sizes
    _, snaps, cells, width = wind_ref.shape
    depth = lon_size // cores
    chips = lat_size * depth
    lat = lax.axis_index("lat")
    lon = lax.axis_index("lon")
    z = lon // cores
    core = lon % cores
    mine = lat * depth + z
    lat_up = (lat + 1) % lat_size
    lat_down = (lat + lat_size - 1) % lat_size
    east = (lon + 1) % lon_size
    west = (lon + lon_size - 1) % lon_size

    def twin(d):
        other = (core + d) % cores
        return other, (lat, z * cores + other)

    def chip(d):
        other = (mine + d) % chips
        return other, (other // depth, (other % depth) * cores + core)

    barrier = pltpu.get_barrier_semaphore()
    def along(d):
        return [(lat, (z + depth + s) % depth * cores + core) for s in (d, -d)]

    strides = relay_strides(depth)
    peers = [
        ((lat + a) % lat_size, z * cores + (core + b) % cores)
        for a in range(lat_size)
        for b in range(cores)
        if a or b
    ]
    peers += [(lat, east), (lat, west)] + (along(1) if depth > 1 else [])
    for peer in peers:
        pl.semaphore_signal(barrier, inc=1, device_id=peer, device_id_type=MESH)

    loads = [
        pltpu.make_async_copy(hbm, wind_ref.at[f], local_sem.at[f])
        for f, hbm in enumerate((u_hbm, v_hbm))
    ]
    for load in loads:
        load.start()
    for load in loads:
        load.wait()

    lane = iota((SUBS, LANES), 1)
    parts = snaps // SUBS
    winds = [[wind_ref[f, :, i, :] for i in range(cells)] for f in range(2)]
    for f in range(2):
        lat_out[0, f] = winds[f][cells - 1]
        lat_out[1, f] = winds[f][0]
    edge = jnp.zeros((SUBS, LANES), jnp.float32)
    for f in range(2):
        for i in range(cells):
            for t in range(parts):
                q = (f * cells + i) * parts + t
                tile = winds[f][i][t * SUBS : (t + 1) * SUBS]
                edge = jnp.where(lane // 2 == q, roll(tile, 2 * q + 1), edge)
    lon_out[...] = edge

    pl.semaphore_wait(barrier, len(peers))

    copies = []
    for way, target in ((0, lat_up), (1, lat_down)):
        copies.append(
            pltpu.make_async_remote_copy(
                src_ref=lat_out.at[way],
                dst_ref=lat_in.at[way],
                send_sem=lat_send.at[way],
                recv_sem=lat_recv.at[way],
                device_id=(target, lon),
                device_id_type=MESH,
            )
        )
    for way, target in ((0, east), (1, west)):
        copies.append(
            pltpu.make_async_remote_copy(
                src_ref=lon_out,
                dst_ref=lon_in.at[way],
                send_sem=lon_send.at[way],
                recv_sem=lon_recv.at[way],
                device_id=(lat, target),
                device_id_type=MESH,
            )
        )
    for at, copy in enumerate(copies):
        if at == 0:
            pl.when(lat < lat_size - 1)(copy.start)
        elif at == 1:
            pl.when(lat > 0)(copy.start)
        else:
            copy.start()

    def relay(at):
        for peer in along(strides[at]):
            pl.semaphore_signal(relay_sem.at[at], inc=1, device_id=peer, device_id_type=MESH)

    if strides:
        relay(0)

    nlat = lat_size * cells
    step = 2.0 * math.pi / (lon_size * width)
    row_index = lat * cells - 1 + iota((2 * SUBS, LANES), 0)
    cosines = jnp.cos((row_index.astype(jnp.float32) + 0.5 - nlat / 2) * step)
    weights = jnp.where((row_index >= 0) & (row_index < nlat), cosines, 0.0)
    scales = 0.5 / jnp.sqrt(cosines)

    def weight(i):
        return weights[i + 1 : i + 2, :]

    def scale(i):
        return scales[i + 1 : i + 2, :]

    wide = iota((snaps, LANES), 1)

    def lon_inner(tile):
        right = jnp.where(wide == LANES - 1, 0.0, pltpu.roll(tile, LANES - 1, 1))
        return right - jnp.where(wide == 0, 0.0, pltpu.roll(tile, 1, 1))

    def lat_inner(f, i):
        high = weight(i + 1) * winds[f][i + 1] if i + 1 < cells else 0.0
        low = weight(i - 1) * winds[f][i - 1] if i > 0 else 0.0
        return high - low

    for i in range(cells):
        x_ref[i] = lon_inner(winds[1][i]) - lat_inner(0, i)
        x_ref[cells + i] = lon_inner(winds[0][i]) + lat_inner(1, i)

    for at in range(1, len(strides)):
        pl.semaphore_wait(relay_sem.at[at - 1], 2)
        relay(at)

    for at, copy in enumerate(copies):
        if at == 0:
            pl.when(lat > 0)(copy.wait_recv)
        elif at == 1:
            pl.when(lat < lat_size - 1)(copy.wait_recv)
        else:
            copy.wait_recv()

    ends = jnp.where(lane % 2 == 1, roll(lon_in[0], 1), roll(lon_in[1], LANES - 1))
    sign = jnp.where(lane == LANES - 1, 1.0, jnp.where(lane == 0, -1.0, 0.0))

    def lon_edge(f, i):
        pieces = []
        for t in range(parts):
            q = (f * cells + i) * parts + t
            pieces.append(sign * roll(ends, -(2 * q + 1)))
        return jnp.concatenate(pieces, axis=0)

    def lat_edge(f, i):
        total = 0.0
        if i == cells - 1:
            total = total + weight(cells) * lat_in[1, f]
        if i == 0:
            total = total - weight(-1) * lat_in[0, f]
        return total

    columns = []
    for i in range(cells):
        columns.append((x_ref[i] + lon_edge(1, i) - lat_edge(0, i)) * scale(i))
    for i in range(cells):
        columns.append((x_ref[cells + i] + lon_edge(0, i) + lat_edge(1, i)) * scale(i))
    block = jnp.concatenate(columns, axis=1)

    pending = []

    def exchange(buf, slot, count, peer_of, send, recv, pair):
        for part in range(2):
            buf[slot, part] = pair[part]
        for d in range(1, count):
            other, peer = peer_of(d)
            copy = pltpu.make_async_remote_copy(
                src_ref=buf.at[slot],
                dst_ref=buf.at[slot],
                send_sem=send,
                recv_sem=recv,
                device_id=peer,
                device_id_type=MESH,
            )
            copy.start()
        arrived = buf.at[pl.ds(0, count - 1)]
        pending.append((arrived, send))
        pltpu.make_async_copy(arrived, arrived, recv).wait()
        totals = [(buf[index, 0], buf[index, 1]) for index in range(count)]
        while len(totals) > 1:
            merged = []
            for at in range(0, len(totals) - 1, 2):
                (a, b), (x, y) = totals[at], totals[at + 1]
                high, low = two_sum(a, x)
                merged.append((high, low + (b + y)))
            if len(totals) % 2:
                merged.append(totals[-1])
            totals = merged
        return two_sum(*totals[0])

    pair = packed_gram(block, snaps)
    if cores > 1:
        pair = exchange(pair_buf, core, cores, twin, pair_send, pair_recv, pair)
    if strides:
        pl.semaphore_wait(relay_sem.at[len(strides) - 1], 2)
    if chips > 1:
        pair = exchange(chip_buf, mine, chips, chip, chip_send, chip_recv, pair)
    high, low = pair

    groups = snaps // SUBS
    sub = iota((SUBS, LANES), 0)
    start = []
    for g in range(groups):
        unit = jnp.where(lane == sub + g * SUBS, 1.0, 0.0)
        start.append(jnp.where(lane < snaps, unit, roll(high, snaps - g * snaps)))
    first, lower = factorize(start, snaps)
    inverse = first[:, :snaps]
    solved = dot(inverse, block, ((1,), (0,)))
    gap = residual(high, low, lower, snaps)
    wide_inverse = jnp.concatenate([jnp.zeros_like(inverse), inverse], axis=0)
    moved = pair_dot(gap, wide_inverse, ((1,), (1,)))
    moved = pair_dot(
        inverse, jnp.concatenate([moved, jnp.zeros_like(moved)], axis=1), ((1,), (0,))
    )
    start = []
    for g in range(groups):
        at = sub + g * SUBS
        unit = jnp.where((lane == at) | (lane == at + snaps), 1.0, 0.0)
        start.append(moved[g * SUBS : (g + 1) * SUBS] + unit)
    second, _ = factorize(start, snaps)
    modes = pair_dot(second[:, :snaps] * root, solved, ((1,), (0,)))
    for f in range(2):
        for i in range(cells):
            at = (f * cells + i) * width
            modes_ref[:, f, i, :] = modes[:, at : at + width]
    factor_ref[...] = dot(second[:, : 2 * snaps], lower[:, : 2 * snaps], ((1,), (1,))) / root

    for at, copy in enumerate(copies):
        if at == 0:
            pl.when(lat < lat_size - 1)(copy.wait_send)
        elif at == 1:
            pl.when(lat > 0)(copy.wait_send)
        else:
            copy.wait_send()
    for sent, send in pending:
        pltpu.make_async_copy(sent, sent, send).wait()


def relay_strides(depth):
    strides, reach = [], 0
    while reach < depth // 2:
        strides.append(max(reach, 1))
        reach += strides[-1]
    return strides


def shards(sizes, wind_u, wind_v):
    snaps, cells, width = wind_u.shape
    lat_size, lon_size, cores = sizes
    chips = lat_size * lon_size // cores
    f32 = jnp.float32
    dma = pltpu.SemaphoreType.DMA
    vmem = pl.BlockSpec(memory_space=pltpu.VMEM)
    hbm = pl.BlockSpec(memory_space=pltpu.HBM)
    root = math.sqrt(2 * lat_size * cells * lon_size * width)
    return pl.pallas_call(
        functools.partial(kernel, sizes, root),
        out_shape=(
            jax.ShapeDtypeStruct((snaps, 2, cells, width), f32),
            jax.ShapeDtypeStruct((snaps, snaps), f32),
        ),
        in_specs=[hbm, hbm],
        out_specs=(vmem, vmem),
        scratch_shapes=[
            pltpu.VMEM((2, snaps, cells, width), f32),
            pltpu.VMEM((2 * cells, snaps, width), f32),
            pltpu.VMEM((2, 2, snaps, width), f32),
            pltpu.VMEM((2, 2, snaps, width), f32),
            pltpu.VMEM((SUBS, LANES), f32),
            pltpu.VMEM((2, SUBS, LANES), f32),
            pltpu.VMEM((cores, 2, SUBS, LANES), f32),
            pltpu.VMEM((chips, 2, SUBS, LANES), f32),
            dma((2,)),
            dma((2,)),
            dma((2,)),
            dma((2,)),
            dma,
            dma,
            dma,
            dma,
            pltpu.SemaphoreType.REGULAR((max(len(relay_strides(lon_size // cores)), 1),)),
            dma((2,)),
        ],
        compiler_params=pltpu.CompilerParams(
            collective_id=0, has_side_effects=True, vmem_limit_bytes=VMEM_BYTES
        ),
    )(*(pltpu.with_memory_space_constraint(w, pltpu.HBM) for w in (wind_u, wind_v)))


def solution(mesh):
    lat_size, lon_size = mesh.shape["lat"], mesh.shape["lon"]
    sizes = (lat_size, lon_size, 2 if lon_size % 2 == 0 else 1)
    in_specs = (P(None, "lat", "lon"), P(None, "lat", "lon"))
    out_specs = (P(None, None, "lat", "lon"), P())
    return jax.shard_map(
        functools.partial(shards, sizes),
        mesh=mesh,
        in_specs=in_specs,
        out_specs=out_specs,
        check_vma=False,
    )
```

```python
import functools
import math

import jax
import jax.numpy as jnp
from jax import lax
from jax.experimental import pallas as pl
from jax.experimental.pallas import tpu as pltpu
from jax.sharding import PartitionSpec as P

MESH = pl.DeviceIdType.MESH
LANES = 128
SUBS = 8
DIRECT = 64
VMEM_BYTES = 8 * 1024 * 1024


def iota(shape, dim):
    return lax.broadcasted_iota(jnp.int32, shape, dim)


def dot(left, right, dims):
    return lax.dot_general(
        left,
        right,
        (dims, ((), ())),
        precision=lax.Precision.HIGHEST,
        preferred_element_type=jnp.float32,
    )


def two(tile):
    high = tile.astype(jnp.bfloat16)
    return high, (tile - high.astype(jnp.float32)).astype(jnp.bfloat16)


def pair_dot(left, right, dims):
    a, b = two(left)
    x, y = two(right)

    def one(m, n):
        return lax.dot_general(m, n, (dims, ((), ())), preferred_element_type=jnp.float32)

    return one(a, x) + (one(a, y) + one(b, x))


def roll(tile, shift):
    shift = shift % LANES
    return tile if shift == 0 else pltpu.roll(tile, shift, 1)


def spread(tile):
    return jnp.broadcast_to(tile, (SUBS, LANES))


def two_sum(a, b):
    total = a + b
    part = total - a
    return total, (a - (total - part)) + (b - part)


def power_above(bound):
    wide = bound * (2.0**23 + 1.0)
    return 2.0 * jnp.abs(wide - wide * (1.0 - 2.0**-24))


def fixed_slices(tile, unit, bits):
    out = []
    for count in bits:
        magic = unit * (1.5 * 2.0 ** (23 - count))
        part = (tile + magic) - magic
        out.append(part.astype(jnp.bfloat16))
        tile = tile - part
    out.append(tile.astype(jnp.bfloat16))
    return out


def factorize(source, n):
    groups = n // SUBS
    lane = iota((SUBS, LANES), 1)
    sub = iota((SUBS, LANES), 0)
    columns = {
        (g, k): spread(source(g, k)) for k in range(n) for g in range(k // SUBS, groups)
    }
    rows = [jnp.where(lane == sub + g * SUBS, 1.0, 0.0) for g in range(groups)]
    pivots = [None] * groups
    lower = [jnp.zeros((SUBS, LANES), jnp.float32)] * groups
    across = jnp.ones((SUBS, LANES), jnp.float32)
    for k in range(n):
        r, s = divmod(k, SUBS)
        pivot = spread(columns[r, k][s : s + 1, :])
        pivots[r] = pivot if s == 0 else jnp.where(sub == s, pivot, pivots[r])
        across = jnp.where(lane == n + k, pivot, across)
        inverse = 1.0 / pivot
        scaled = {g: columns[g, k] * inverse for g in range(r, groups)}
        for j in range(k + 1, n):
            head = spread(columns[j // SUBS, k][j % SUBS : j % SUBS + 1, :])
            for g in range(j // SUBS, groups):
                columns[g, j] = columns[g, j] - scaled[g] * head
        pivot_row = spread(rows[r][s : s + 1, :])
        for g in range(r, groups):
            lower[g] = jnp.where(lane == n + k, columns[g, k], lower[g])
            factor = scaled[g]
            if g == r:
                if s == SUBS - 1:
                    continue
                factor = jnp.where(sub > s, factor, 0.0)
            rows[g] = rows[g] - factor * pivot_row
    across = 1.0 / jnp.sqrt(across)
    out, left = [], []
    for g in range(groups):
        out.append(rows[g] * (1.0 / jnp.sqrt(pivots[g])))
        keep = (lane >= n) & (lane - n - g * SUBS <= sub)
        left.append(jnp.where(keep, lower[g] * across, 0.0))
    return jnp.concatenate(out, axis=0), jnp.concatenate(left, axis=0)


def packed_gram(block, n):
    groups = n // SUBS
    peak = jnp.max(jnp.abs(block), axis=1, keepdims=True)
    unit = power_above(jnp.broadcast_to(peak, (n, LANES)))
    pieces = []
    for at in range(0, block.shape[1], LANES):
        pieces.append(fixed_slices(block[:, at : at + LANES], unit, (5, 12, 19)))
    stack = jnp.concatenate(
        [jnp.concatenate([piece[a] for piece in pieces], axis=1) for a in range(4)], axis=0
    )
    gram = lax.dot_general(
        stack, stack, (((1,), (1,)), ((), ())), preferred_element_type=jnp.float32
    )
    quarter = iota((SUBS, LANES), 1) // n

    def tile(a, g):
        at = a * n + g * SUBS
        return roll(gram[at : at + SUBS], a * n)

    near, far = [], []
    for g in range(groups):
        turned = [tile(a, g) for a in range(4)]
        held = [turned[0]] + [jnp.where(quarter >= a, turned[a], 0.0) for a in range(1, 4)]
        past = [jnp.where(quarter < a, turned[a], 0.0) for a in range(1, 4)]
        near.append((held[0] + held[3]) + (held[1] + held[2]))
        far.append((past[0] + past[2]) + past[1])

    def gather(tiles, order):
        total = None
        for g in range(groups):
            moved = roll(tiles[g], n * (g - order))
            total = moved if total is None else jnp.where(quarter == g, moved, total)
        return total

    order = [gather(near, o) for o in range(4)]
    rest = gather(far, 0) + (gather(far, 1) + gather(far, 2))
    high, low = two_sum(order[0], order[1])
    high, more = two_sum(high, order[2])
    high, low = two_sum(high, (low + more) + (order[3] + rest))
    ahead = place(n)
    edge = jnp.sum(jnp.where(ahead == 0, low, 0.0), axis=0, keepdims=True)
    return jnp.where(ahead > 0, low, high), edge


def place(n):
    lane = iota((SUBS, LANES), 1)
    return lane % n - (lane // n * SUBS + iota((SUBS, LANES), 0))


def residual(total, error, edge, lower, n):
    groups = n // SUBS
    shape = (n, n)
    row, col = iota(shape, 0), iota(shape, 1)

    def unpack(packed):
        return jnp.concatenate([roll(packed, -g * n) for g in range(groups)], axis=0)

    def flip(tile):
        return jnp.transpose(tile)[:n]

    whole, rest = unpack(total), unpack(error)
    whole_flip, rest_flip = flip(whole)[:, :n], flip(rest)[:, :n]
    whole, rest = whole[:, :n], rest[:, :n]
    diagonal = jnp.zeros((1, LANES), jnp.float32)
    lane = iota((1, LANES), 1)
    for g in range(groups):
        diagonal = jnp.where(lane // SUBS == g, roll(edge, -g * n), diagonal)
    diagonal = jnp.broadcast_to(diagonal[:, :n], shape)
    high = jnp.where(row >= col, whole, whole_flip)
    low = jnp.where(row > col, rest + whole_flip, rest_flip + whole)
    low = jnp.where(row == col, rest + diagonal, low)
    peak = jnp.sqrt(jnp.sum(jnp.where(row == col, high, 0.0), axis=1, keepdims=True)) * 1.01
    unit = power_above(jnp.broadcast_to(peak, (n, LANES)))
    slices = fixed_slices(lower, unit, (8, 17, 26))
    stack = jnp.concatenate(slices, axis=0)
    products = [
        lax.dot_general(
            stack[:, : 2 * n],
            one[:, : 2 * n],
            (((1,), (1,)), ((), ())),
            preferred_element_type=jnp.float32,
        )
        for one in slices
    ]

    def order(count):
        total = None
        for a in range(4):
            b = count - a
            if 0 <= b < 4:
                one = products[b][a * n : (a + 1) * n]
                total = one if total is None else total + one
        return total

    first, low_one = two_sum(high, -order(0))
    first, low_two = two_sum(first, -order(1))
    first, low_three = two_sum(first, -order(2))
    tail = (low_one + low_two) + (low_three + (low - (order(3) + (order(4) + order(5)))))
    return first + tail


def kernel(
    sizes,
    root,
    u_hbm,
    v_hbm,
    solved_ref,
    turn_ref,
    factor_ref,
    wind_ref,
    x_ref,
    hold_ref,
    lat_in,
    lon_out,
    lon_in,
    sum_bufs,
    lat_send,
    lat_recv,
    lon_send,
    lon_recv,
    sum_send,
    sum_recv,
    relay_sem,
    local_sem,
):
    lat_size, lon_size, cores = sizes
    _, cells, snaps, width = wind_ref.shape
    depth = lon_size // cores
    chips = lat_size * depth
    lat = lax.axis_index("lat")
    lon = lax.axis_index("lon")
    z = lon // cores
    core = lon % cores
    mine = lat * depth + z
    lat_up = (lat + 1) % lat_size
    lat_down = (lat + lat_size - 1) % lat_size
    east = (lon + 1) % lon_size
    west = (lon + lon_size - 1) % lon_size

    loads = [
        pltpu.make_async_copy(hbm.at[:, i], wind_ref.at[f, i], local_sem)
        for f, hbm in enumerate((u_hbm, v_hbm))
        for i in range(cells)
    ]
    for load in loads:
        load.start()

    barrier = pltpu.get_barrier_semaphore()

    def along(d):
        return [(lat, (z + depth + s) % depth * cores + core) for s in (d, -d)]

    strides = relay_strides(depth)
    peers = [
        ((lat + a) % lat_size, z * cores + (core + b) % cores)
        for a in range(lat_size)
        for b in range(cores)
        if a or b
    ]
    peers += [(lat, east), (lat, west)] + (along(1) if depth > 1 else [])
    for peer in peers:
        pl.semaphore_signal(barrier, inc=1, device_id=peer, device_id_type=MESH)

    pltpu.make_async_copy(wind_ref, wind_ref, local_sem).wait()

    lane = iota((SUBS, LANES), 1)
    parts = snaps // SUBS
    winds = [[wind_ref[f, i] for i in range(cells)] for f in range(2)]
    edges = [jnp.zeros((SUBS, LANES), jnp.float32)] * parts
    for f in range(2):
        for i in range(cells):
            for t in range(parts):
                q = (f * cells + i) * parts + t
                tile = winds[f][i][t * SUBS : (t + 1) * SUBS]
                edges[t] = jnp.where(lane // 2 == q, roll(tile, 2 * q + 1), edges[t])
    while len(edges) > 1:
        edges = [sum(edges[at : at + 2]) for at in range(0, len(edges), 2)]
    lon_out[...] = edges[0]

    pl.semaphore_wait(barrier, len(peers))

    copies = []
    for way, target in ((0, lat_up), (1, lat_down)):
        copies.append(
            pltpu.make_async_remote_copy(
                src_ref=wind_ref.at[:, 0 if way else cells - 1],
                dst_ref=lat_in.at[way],
                send_sem=lat_send.at[way],
                recv_sem=lat_recv.at[way],
                device_id=(target, lon),
                device_id_type=MESH,
            )
        )
    for way, target in ((0, east), (1, west)):
        copies.append(
            pltpu.make_async_remote_copy(
                src_ref=lon_out,
                dst_ref=lon_in.at[way],
                send_sem=lon_send.at[way],
                recv_sem=lon_recv.at[way],
                device_id=(lat, target),
                device_id_type=MESH,
            )
        )
    for at, copy in enumerate(copies):
        if at == 0:
            pl.when(lat < lat_size - 1)(copy.start)
        elif at == 1:
            pl.when(lat > 0)(copy.start)
        else:
            copy.start()

    def relay(at):
        for peer in along(strides[at]):
            pl.semaphore_signal(relay_sem.at[at], inc=1, device_id=peer, device_id_type=MESH)

    if strides:
        relay(0)

    nlat = lat_size * cells
    step = 2.0 * math.pi / (lon_size * width)
    row_index = lat * cells - 1 + iota((2 * SUBS, LANES), 0)
    cosines = jnp.cos((row_index.astype(jnp.float32) + 0.5 - nlat / 2) * step)
    weights = jnp.where((row_index >= 0) & (row_index < nlat), cosines, 0.0)
    scales = 0.5 / jnp.sqrt(cosines)

    def weight(i):
        return weights[i + 1 : i + 2, :]

    def scale(i):
        return scales[i + 1 : i + 2, :]

    wide = iota((snaps, LANES), 1)

    def lon_inner(tile):
        right = jnp.where(wide == LANES - 1, 0.0, pltpu.roll(tile, LANES - 1, 1))
        return right - jnp.where(wide == 0, 0.0, pltpu.roll(tile, 1, 1))

    def lat_inner(f, i):
        high = weight(i + 1) * winds[f][i + 1] if i + 1 < cells else 0.0
        low = weight(i - 1) * winds[f][i - 1] if i > 0 else 0.0
        return high - low

    for i in range(cells):
        x_ref[i] = lon_inner(winds[1][i]) - lat_inner(0, i)
        x_ref[cells + i] = lon_inner(winds[0][i]) + lat_inner(1, i)

    for at in range(1, len(strides)):
        pl.semaphore_wait(relay_sem.at[at - 1], 2)
        relay(at)

    for at, copy in enumerate(copies):
        if at == 0:
            pl.when(lat > 0)(copy.wait_recv)
        elif at == 1:
            pl.when(lat < lat_size - 1)(copy.wait_recv)
        else:
            copy.wait_recv()

    ends = jnp.where(lane % 2 == 1, roll(lon_in[0], 1), roll(lon_in[1], LANES - 1))
    sign = jnp.where(lane == LANES - 1, 1.0, jnp.where(lane == 0, -1.0, 0.0))

    def lon_edge(f, i):
        pieces = []
        for t in range(parts):
            q = (f * cells + i) * parts + t
            pieces.append(sign * roll(ends, -(2 * q + 1)))
        return jnp.concatenate(pieces, axis=0)

    def lat_edge(f, i):
        total = 0.0
        if i == cells - 1:
            total = total + weight(cells) * lat_in[1, f]
        if i == 0:
            total = total - weight(-1) * lat_in[0, f]
        return total

    columns = []
    for i in range(cells):
        columns.append((x_ref[i] + lon_edge(1, i) - lat_edge(0, i)) * scale(i))
    for i in range(cells):
        columns.append((x_ref[cells + i] + lon_edge(0, i) + lat_edge(1, i)) * scale(i))
    block = jnp.concatenate(columns, axis=1)

    pending = []

    def exchange(buf, slot, count, target, at, parts):
        rows = 0
        for part in parts:
            buf[slot, pl.ds(rows, part.shape[0])] = part
            rows += part.shape[0]
        for d in peer_order(count):
            copy = pltpu.make_async_remote_copy(
                src_ref=buf.at[slot],
                dst_ref=buf.at[slot],
                send_sem=sum_send.at[at],
                recv_sem=sum_recv.at[at],
                device_id=target(shifted(slot, d, count)),
                device_id_type=pl.DeviceIdType.LOGICAL,
            )
            copy.start()
        arrived = buf.at[pl.ds(0, count - 1)]
        pending.append((arrived, sum_send.at[at]))
        pltpu.make_async_copy(arrived, arrived, sum_recv.at[at]).wait()
        edges = [buf[index, pl.ds(SUBS, 1)] for index in range(count)]
        while len(edges) > 1:
            edges = [sum(edges[at : at + 2]) for at in range(0, len(edges), 2)]
        zero = jnp.zeros((SUBS, LANES), jnp.float32)
        totals = []
        for index in range(count):
            error = buf[index, pl.ds(SUBS + 1, SUBS)] if len(parts) > 2 else zero
            totals.append((buf[index, pl.ds(0, SUBS)], error))
        while len(totals) > 1:
            merged = []
            for at in range(0, len(totals) - 1, 2):
                (a, b), (x, y) = totals[at], totals[at + 1]
                high, low = two_sum(a, x)
                merged.append((high, low + (b + y)))
            if len(totals) % 2:
                merged.append(totals[-1])
            totals = merged
        return totals[0][0], edges[0], totals[0][1]

    parts = packed_gram(block, snaps)
    if strides:
        pl.semaphore_wait(relay_sem.at[len(strides) - 1], 2)
    if len(sum_bufs) == 1:
        everyone = lat_size * lon_size
        parts = exchange(sum_bufs[0], lat * lon_size + lon, everyone, lambda at: at, 0, parts)
    else:
        parts = exchange(sum_bufs[0], lon, lon_size, lambda at: lat * lon_size + at, 0, parts)
        parts = exchange(sum_bufs[1], lat, lat_size, lambda at: at * lon_size + lon, 1, parts)
    local, edge, error = parts
    ahead = place(snaps)
    total, error = two_sum(local, error)
    total = jnp.where(ahead > 0, total + error, total)
    error = jnp.where(ahead > 0, 0.0, error)

    groups = snaps // SUBS
    sub = iota((SUBS, LANES), 0)
    first, lower = factorize(
        lambda g, k: total[:, g * snaps + k : g * snaps + k + 1], snaps
    )
    inverse = first[:, :snaps]
    hold_ref[0] = first
    gap = residual(total, error, edge, lower, snaps)
    moved = pair_dot(gap, inverse, ((1,), (1,)))
    moved = pair_dot(inverse, moved, ((1,), (0,)))
    start = []
    for g in range(groups):
        at = iota((SUBS, snaps), 0) + g * SUBS
        unit = jnp.where(iota((SUBS, snaps), 1) == at, 1.0, 0.0)
        start.append(moved[g * SUBS : (g + 1) * SUBS] + unit)
    hold_ref[1, :, :snaps] = moved

    for at, copy in enumerate(copies):
        if at == 0:
            pl.when(lat < lat_size - 1)(copy.wait_send)
        elif at == 1:
            pl.when(lat > 0)(copy.wait_send)
        else:
            copy.wait_send()
    for sent, send in pending:
        pltpu.make_async_copy(sent, sent, send).wait()

    solved = dot(hold_ref[0][:, :snaps], block, ((1,), (0,)))
    for at, part in enumerate(two(solved)):
        solved_ref[at * snaps : (at + 1) * snaps, :] = part
    second, lower_two = factorize(lambda g, k: start[g][:, k : k + 1], snaps)
    turned = jnp.where(iota((snaps, LANES), 1) < snaps, second * root, 0.0)
    bulk = turned.astype(jnp.bfloat16).astype(jnp.float32)
    rest = turned - bulk
    turn_ref[...] = bulk + pltpu.roll(bulk, snaps, 1) + pltpu.roll(rest, 2 * snaps, 1)
    factor_ref[0] = lower
    factor_ref[1] = lower_two


def shifted(me, d, count):
    if count & (count - 1) == 0:
        return me ^ d
    return (me + d) % count


def peer_order(count):
    return sorted(range(1, count), key=lambda d: (-((d >> 1) & 3), -(d >> 3), d))


def finish(root, solved_ref, turn_ref, lower_ref, modes_hbm, factor_hbm, modes_ref, flat_ref, sem):
    snaps, _, cells, width = modes_hbm.shape
    left = turn_ref[...][:, : 3 * snaps].astype(jnp.bfloat16)
    stores = []
    for f in range(2):
        for i in range(0, cells, 2):
            at = (f * cells + i) * width
            both = solved_ref[:, at : at + 2 * width]
            right = jnp.concatenate([both, both[:snaps]], axis=0)
            modes = lax.dot_general(
                left, right, (((1,), (0,)), ((), ())), preferred_element_type=jnp.float32
            )
            for c in range(2):
                modes_ref[f, i + c] = modes[:, c * width : (c + 1) * width]
                stores.append(
                    pltpu.make_async_copy(modes_ref.at[f, i + c], modes_hbm.at[:, f, i + c], sem)
                )
                stores[-1].start()
    lower, lower_two = lower_ref[0], lower_ref[1]
    shape = (snaps, LANES)
    lower_two = pltpu.roll(lower_two, LANES - snaps, 1)
    wide = jnp.concatenate([jnp.zeros((snaps, LANES), jnp.float32), lower_two], axis=0)
    flat = dot(lower[:, : 2 * snaps], wide, ((1,), (0,))) / root
    flat_ref[...] = jnp.transpose(flat)[:snaps, :snaps]
    stores.append(pltpu.make_async_copy(flat_ref, factor_hbm, sem))
    stores[-1].start()
    for store in stores:
        store.wait()


def relay_strides(depth):
    strides, reach = [], 0
    while reach < depth // 2:
        strides.append(max(reach, 1))
        reach += strides[-1]
    return strides


def shards(sizes, wind_u, wind_v):
    snaps, cells, width = wind_u.shape
    lat_size, lon_size, cores = sizes
    chips = lat_size * lon_size // cores
    f32 = jnp.float32
    dma = pltpu.SemaphoreType.DMA
    vmem = pl.BlockSpec(memory_space=pltpu.VMEM)
    hbm = pl.BlockSpec(memory_space=pltpu.HBM)
    root = math.sqrt(2 * lat_size * cells * lon_size * width)
    if lat_size * lon_size <= DIRECT:
        sum_bufs = [pltpu.VMEM((lat_size * lon_size, SUBS + 1, LANES), f32)]
    else:
        sum_bufs = [
            pltpu.VMEM((lon_size, SUBS + 1, LANES), f32),
            pltpu.VMEM((lat_size, 2 * SUBS + 1, LANES), f32),
        ]
    held = pl.pallas_call(
        functools.partial(kernel, sizes, root),
        out_shape=(
            pltpu.VMEM((2 * snaps, 2 * cells * width), jnp.bfloat16),
            pltpu.VMEM((snaps, LANES), f32),
            pltpu.VMEM((2, snaps, LANES), f32),
        ),
        in_specs=[hbm, hbm],
        out_specs=(vmem, vmem, vmem),
        scratch_shapes=[
            pltpu.VMEM((2, cells, snaps, width), f32),
            pltpu.VMEM((2 * cells, snaps, width), f32),
            pltpu.VMEM((2, snaps, LANES), f32),
            pltpu.VMEM((2, 2, snaps, width), f32),
            pltpu.VMEM((SUBS, LANES), f32),
            pltpu.VMEM((2, SUBS, LANES), f32),
            sum_bufs,
            dma((2,)),
            dma((2,)),
            dma((2,)),
            dma((2,)),
            dma((len(sum_bufs),)),
            dma((len(sum_bufs),)),
            pltpu.SemaphoreType.REGULAR((max(len(relay_strides(lon_size // cores)), 1),)),
            dma,
        ],
        compiler_params=pltpu.CompilerParams(
            collective_id=0, has_side_effects=True, vmem_limit_bytes=VMEM_BYTES
        ),
    )(*(pltpu.with_memory_space_constraint(w, pltpu.HBM) for w in (wind_u, wind_v)))
    anywhere = pl.BlockSpec(memory_space=pl.ANY)
    return pl.pallas_call(
        functools.partial(finish, root),
        out_shape=(
            jax.ShapeDtypeStruct((snaps, 2, cells, width), f32),
            jax.ShapeDtypeStruct((snaps, snaps), f32),
        ),
        in_specs=[vmem, vmem, vmem],
        out_specs=(anywhere, anywhere),
        scratch_shapes=[
            pltpu.VMEM((2, cells, snaps, width), f32),
            pltpu.VMEM((snaps, snaps), f32),
            dma,
        ],
        compiler_params=pltpu.CompilerParams(vmem_limit_bytes=VMEM_BYTES),
    )(*held)


def solution(mesh):
    lat_size, lon_size = mesh.shape["lat"], mesh.shape["lon"]
    sizes = (lat_size, lon_size, 2 if lon_size % 2 == 0 else 1)
    in_specs = (P(None, "lat", "lon"), P(None, "lat", "lon"))
    out_specs = (P(None, None, "lat", "lon"), P())
    return jax.shard_map(
        functools.partial(shards, sizes),
        mesh=mesh,
        in_specs=in_specs,
        out_specs=out_specs,
        check_vma=False,
    )
```

```python
import functools
import math

import jax
import jax.numpy as jnp
from jax import lax
from jax.experimental import pallas as pl
from jax.experimental.pallas import tpu as pltpu
from jax.sharding import PartitionSpec as P

MESH = pl.DeviceIdType.MESH
LANES = 128
SUBS = 8
DIRECT = 64
VMEM_BYTES = 8 * 1024 * 1024


def iota(shape, dim):
    return lax.broadcasted_iota(jnp.int32, shape, dim)


def dot(left, right, dims):
    return lax.dot_general(
        left,
        right,
        (dims, ((), ())),
        precision=lax.Precision.HIGHEST,
        preferred_element_type=jnp.float32,
    )


def two(tile):
    high = tile.astype(jnp.bfloat16)
    return high, (tile - high.astype(jnp.float32)).astype(jnp.bfloat16)


def three(tile):
    high = tile.astype(jnp.bfloat16)
    tile = tile - high.astype(jnp.float32)
    return (high,) + two(tile)


def pair_dot(left, right, dims):
    a, b = two(left)
    x, y = two(right)

    def one(m, n):
        return lax.dot_general(m, n, (dims, ((), ())), preferred_element_type=jnp.float32)

    return one(a, x) + (one(a, y) + one(b, x))


def roll(tile, shift):
    shift = shift % LANES
    return tile if shift == 0 else pltpu.roll(tile, shift, 1)


def spread(tile):
    return jnp.broadcast_to(tile, (SUBS, LANES))


def two_sum(a, b):
    total = a + b
    part = total - a
    return total, (a - (total - part)) + (b - part)


def power_above(bound):
    wide = bound * (2.0**23 + 1.0)
    return 2.0 * jnp.abs(wide - wide * (1.0 - 2.0**-24))


def fixed_slices(tile, unit, bits):
    out = []
    for count in bits:
        magic = unit * (1.5 * 2.0 ** (23 - count))
        part = (tile + magic) - magic
        out.append(part.astype(jnp.bfloat16))
        tile = tile - part
    out.append(tile.astype(jnp.bfloat16))
    return out


def factorize(source, upper, n):
    groups = n // SUBS
    lane = iota((SUBS, LANES), 1)
    sub = iota((SUBS, LANES), 0)
    columns = {}

    def bring(first, last, take):
        for k in range(first * SUBS, min(last, groups) * SUBS):
            for g in range(k // SUBS, groups):
                columns[g, k] = spread(take(g, k))

    bring(0, 2, source)
    upper = list(upper)
    rows = [jnp.where(lane == sub + g * SUBS, 1.0, 0.0) for g in range(groups)]
    pivots = [None] * groups
    lower = [jnp.zeros((SUBS, LANES), jnp.float32)] * groups
    across = jnp.ones((SUBS, LANES), jnp.float32)
    for k in range(n):
        r, s = divmod(k, SUBS)
        if s == 0 and r > 0:
            bring(r + 1, r + 2, lambda g, j: upper[g][:, j : j + 1])
        pivot = spread(columns[r, k][s : s + 1, :])
        pivots[r] = pivot if s == 0 else jnp.where(sub == s, pivot, pivots[r])
        across = jnp.where(lane == n + k, pivot, across)
        inverse = 1.0 / pivot
        scaled = {g: columns[g, k] * inverse for g in range(r, groups)}
        for j in range(k + 1, min(n, (r + 2) * SUBS)):
            head = spread(columns[j // SUBS, k][j % SUBS : j % SUBS + 1, :])
            for g in range(j // SUBS, groups):
                columns[g, j] = columns[g, j] - scaled[g] * head
        pivot_row = spread(rows[r][s : s + 1, :])
        upper_row = jnp.broadcast_to(upper[r][s : s + 1, :], upper[r].shape)
        for g in range(r, groups):
            lower[g] = jnp.where(lane == n + k, columns[g, k], lower[g])
            factor = scaled[g]
            if g == r:
                if s == SUBS - 1:
                    continue
                factor = jnp.where(sub > s, factor, 0.0)
            rows[g] = rows[g] - factor * pivot_row
            if r + 2 < groups:
                upper[g] = upper[g] - factor[:, : upper_row.shape[1]] * upper_row
    across = 1.0 / jnp.sqrt(across)
    out, left = [], []
    for g in range(groups):
        out.append(rows[g] * (1.0 / jnp.sqrt(pivots[g])))
        keep = (lane >= n) & (lane - n - g * SUBS <= sub)
        left.append(jnp.where(keep, lower[g] * across, 0.0))
    return jnp.concatenate(out, axis=0), jnp.concatenate(left, axis=0)


def gram_pair(tiles, n):
    groups = n // SUBS
    peak = jnp.max(functools.reduce(jnp.maximum, map(jnp.abs, tiles)), axis=1, keepdims=True)
    unit = power_above(jnp.broadcast_to(peak, (n, LANES)))
    pieces = [fixed_slices(tile, unit, (5, 12, 19)) for tile in tiles]
    stack = jnp.concatenate(
        [jnp.concatenate([piece[a] for piece in pieces], axis=1) for a in range(4)], axis=0
    )
    gram = lax.dot_general(
        stack, stack, (((1,), (1,)), ((), ())), preferred_element_type=jnp.float32
    )
    quarter = iota((SUBS, LANES), 1) // n

    def tile(a, g):
        at = a * n + g * SUBS
        return roll(gram[at : at + SUBS], a * n)

    near, far = [], []
    for g in range(groups):
        turned = [tile(a, g) for a in range(4)]
        held = [turned[0]] + [jnp.where(quarter >= a, turned[a], 0.0) for a in range(1, 4)]
        past = [jnp.where(quarter < a, turned[a], 0.0) for a in range(1, 4)]
        near.append((held[0] + held[3]) + (held[1] + held[2]))
        far.append((past[0] + past[2]) + past[1])

    def gather(tiles, order):
        total = None
        for g in range(groups):
            moved = roll(tiles[g], n * (g - order))
            total = moved if total is None else jnp.where(quarter == g, moved, total)
        return total

    order = [gather(near, o) for o in range(4)]
    rest = gather(far, 0) + (gather(far, 1) + gather(far, 2))
    high, low = two_sum(order[0], order[1])
    high, more = two_sum(high, order[2])
    return two_sum(high, (low + more) + (order[3] + rest))


def message(high, low, n):
    ahead = place(n)
    edge = jnp.sum(jnp.where(ahead == 0, low, 0.0), axis=0, keepdims=True)
    return jnp.where(ahead > 0, low, high), edge


def place(n):
    lane = iota((SUBS, LANES), 1)
    return lane % n - (lane // n * SUBS + iota((SUBS, LANES), 0))


def restore(total, error, edge, n):
    groups = n // SUBS
    shape = (n, n)
    row, col = iota(shape, 0), iota(shape, 1)

    def unpack(packed):
        return jnp.concatenate([roll(packed, -g * n) for g in range(groups)], axis=0)

    def flip(tile):
        return jnp.transpose(tile)[:n]

    whole, rest = unpack(total), unpack(error)
    whole_flip, rest_flip = flip(whole)[:, :n], flip(rest)[:, :n]
    whole, rest = whole[:, :n], rest[:, :n]
    diagonal = jnp.zeros((1, LANES), jnp.float32)
    lane = iota((1, LANES), 1)
    for g in range(groups):
        diagonal = jnp.where(lane // SUBS == g, roll(edge, -g * n), diagonal)
    diagonal = jnp.broadcast_to(diagonal[:, :n], shape)
    high = jnp.where(row >= col, whole, whole_flip)
    low = jnp.where(row > col, rest + whole_flip, rest_flip + whole)
    return high, jnp.where(row == col, rest + diagonal, low)


def residual(high, low, lower, n):
    row, col = iota((n, n), 0), iota((n, n), 1)
    peak = jnp.sqrt(jnp.sum(jnp.where(row == col, high, 0.0), axis=1, keepdims=True)) * 1.01
    unit = power_above(jnp.broadcast_to(peak, (n, LANES)))
    slices = fixed_slices(lower, unit, (8, 17, 26))
    stack = jnp.concatenate(slices, axis=0)
    products = [
        lax.dot_general(
            stack[:, : 2 * n],
            one[:, : 2 * n],
            (((1,), (1,)), ((), ())),
            preferred_element_type=jnp.float32,
        )
        for one in slices
    ]

    def order(count):
        total = None
        for a in range(4):
            b = count - a
            if 0 <= b < 4:
                one = products[b][a * n : (a + 1) * n]
                total = one if total is None else total + one
        return total

    first, low_one = two_sum(high, -order(0))
    first, low_two = two_sum(first, -order(1))
    first, low_three = two_sum(first, -order(2))
    tail = (low_one + low_two) + (low_three + (low - (order(3) + (order(4) + order(5)))))
    return first + tail


def kernel(
    sizes,
    root,
    u_hbm,
    v_hbm,
    solved_ref,
    turn_ref,
    factor_ref,
    wind_ref,
    x_ref,
    hold_ref,
    ends_ref,
    inner_ref,
    lat_in,
    lon_out,
    lon_in,
    x_parts,
    sum_bufs,
    lat_send,
    lat_recv,
    lon_send,
    lon_recv,
    sum_send,
    sum_recv,
    up_sem,
    down_sem,
    local_sem,
):
    lat_size, lon_size, cores = sizes
    _, cells, snaps, width = wind_ref.shape
    depth = lon_size // cores
    chips = lat_size * depth
    lat = lax.axis_index("lat")
    lon = lax.axis_index("lon")
    z = lon // cores
    core = lon % cores
    mine = lat * depth + z
    lat_up = (lat + 1) % lat_size
    lat_down = (lat + lat_size - 1) % lat_size
    east = (lon + 1) % lon_size
    west = (lon + lon_size - 1) % lon_size

    barrier = pltpu.get_barrier_semaphore()

    first_z, last_z = z == 0, z == depth - 1
    below, above = lon - cores, lon + cores
    ring = [(lat, east), (lat, west)]
    if cores == 2:
        ring = [(lat, (lon + lon_size + 2 * core - 1) % lon_size)]
    around = [
        ((lat + a) % lat_size, z * cores + (core + b) % cores)
        for a in range(lat_size)
        for b in range(cores)
        if a or b
    ]

    def greet(peer):
        pl.semaphore_signal(barrier, inc=1, device_id=peer, device_id_type=MESH)

    for peer in ring + around:
        greet(peer)
    pl.when(jnp.logical_not(first_z))(lambda: greet((lat, below)))
    pl.when(jnp.logical_not(last_z))(lambda: greet((lat, above)))
    callers = len(ring + around) + jnp.where(first_z, 0, 1) + jnp.where(last_z, 0, 1)

    loads = [
        pltpu.make_async_copy(hbm.at[:, i], wind_ref.at[f, i], local_sem)
        for f, hbm in enumerate((u_hbm, v_hbm))
        for i in range(cells)
    ]
    for load in loads:
        load.start()

    pltpu.make_async_copy(wind_ref, wind_ref, local_sem).wait()

    lane = iota((SUBS, LANES), 1)
    parts = snaps // SUBS
    winds = [[wind_ref[f, i] for i in range(cells)] for f in range(2)]
    edges = [jnp.zeros((SUBS, LANES), jnp.float32)] * parts
    for f in range(2):
        for i in range(cells):
            for t in range(parts):
                q = (t * 2 + 1 - f) * cells + i
                tile = winds[f][i][t * SUBS : (t + 1) * SUBS]
                edges[t] = jnp.where(lane // 2 == q, roll(tile, 2 * q + 1), edges[t])
    while len(edges) > 1:
        edges = [sum(edges[at : at + 2]) for at in range(0, len(edges), 2)]
    lon_out[...] = edges[0]

    pl.semaphore_wait(barrier, callers)

    copies = []
    for way, target in ((0, lat_up), (1, lat_down)):
        copies.append(
            pltpu.make_async_remote_copy(
                src_ref=wind_ref.at[:, 0 if way else cells - 1],
                dst_ref=lat_in.at[way],
                send_sem=lat_send.at[way],
                recv_sem=lat_recv.at[way],
                device_id=(target, lon),
                device_id_type=MESH,
            )
        )
    for way, target in ((0, east), (1, west)):
        copies.append(
            pltpu.make_async_remote_copy(
                src_ref=lon_out,
                dst_ref=lon_in.at[way],
                send_sem=lon_send.at[way],
                recv_sem=lon_recv.at[way],
                device_id=(lat, target),
                device_id_type=MESH,
            )
        )
    for at, copy in enumerate(copies):
        if at == 0:
            pl.when(lat < lat_size - 1)(copy.start)
        elif at == 1:
            pl.when(lat > 0)(copy.start)
        else:
            copy.start()

    upper_core, lower_core = core == cores - 1, core == 0

    def tell(sem, targets):
        for target in targets:
            pl.semaphore_signal(sem, inc=1, device_id=(lat, target), device_id_type=MESH)

    def ascend():
        tell(up_sem, [above, east] if cores > 1 else [above])

    def descend():
        tell(down_sem, [below, west] if cores > 1 else [below])

    if depth > 1:
        pl.when(jnp.logical_and(first_z, upper_core))(ascend)
        pl.when(jnp.logical_and(last_z, lower_core))(descend)

    nlat = lat_size * cells
    step = 2.0 * math.pi / (lon_size * width)
    row_index = lat * cells - 1 + iota((2 * SUBS, LANES), 0)
    cosines = jnp.cos((row_index.astype(jnp.float32) + 0.5 - nlat / 2) * step)
    weights = jnp.where((row_index >= 0) & (row_index < nlat), cosines, 0.0)
    scales = 0.5 / jnp.sqrt(cosines)

    def weight(i):
        return weights[i + 1 : i + 2, :]

    def scale(i):
        return scales[i + 1 : i + 2, :]

    wide = iota((snaps, LANES), 1)

    def lon_inner(tile):
        right = jnp.where(wide == LANES - 1, 0.0, pltpu.roll(tile, LANES - 1, 1))
        return right - jnp.where(wide == 0, 0.0, pltpu.roll(tile, 1, 1))

    def lat_inner(f, i):
        high = weight(i + 1) * winds[f][i + 1] if i + 1 < cells else 0.0
        low = weight(i - 1) * winds[f][i - 1] if i > 0 else 0.0
        return high - low

    def inner(f, i):
        if f == 0:
            return lon_inner(winds[1][i]) - lat_inner(0, i)
        return lon_inner(winds[0][i]) + lat_inner(1, i)

    sides = sorted({0, cells - 1})
    middle = [i for i in range(cells) if i not in sides]
    inside = (wide > 0) & (wide < LANES - 1)
    rows_of = 2 * 2 * cells

    def take_ends(tile, f, i, held):
        at = f * cells + i
        out = []
        for t in range(parts):
            moved = roll(tile[t * SUBS : (t + 1) * SUBS], 2 * at + 1)
            out.append(held[t] + jnp.where(lane // 2 == at, moved, 0.0))
        return out

    held = [jnp.zeros((SUBS, LANES), jnp.float32)] * parts
    tiles = []
    for f in range(2):
        for i in middle:
            tile = inner(f, i) * scale(i)
            x_ref[f * cells + i] = tile
            held = take_ends(tile, f, i, held)
            tiles.append(jnp.where(inside, tile, 0.0))
        for i in sides:
            x_ref[f * cells + i] = inner(f, i)
    for t in range(parts):
        ends_ref[t] = held[t]
    if middle:
        high, low = gram_pair(tiles, snaps)
        inner_ref[0] = high
        inner_ref[1] = low

    if depth > 1:
        @pl.when(jnp.logical_not(first_z))
        def _():
            pl.semaphore_wait(up_sem, 1)
            pl.when(jnp.logical_and(upper_core, jnp.logical_not(last_z)))(ascend)

        @pl.when(jnp.logical_not(last_z))
        def _():
            pl.semaphore_wait(down_sem, 1)
            pl.when(jnp.logical_and(lower_core, jnp.logical_not(first_z)))(descend)

    for at, copy in enumerate(copies):
        if at == 0:
            pl.when(lat > 0)(copy.wait_recv)
        elif at == 1:
            pl.when(lat < lat_size - 1)(copy.wait_recv)
        else:
            copy.wait_recv()

    across = jnp.zeros((SUBS, LANES), jnp.float32)
    for i in range(cells):
        across = jnp.where(lane // 2 % cells == i, scale(i), across)
    across = jnp.where(lane < rows_of, across, 0.0)
    ends = []
    for t in range(parts):
        from_east = roll(lon_in[1], -1 - t * rows_of)
        from_west = roll(lon_in[0], 1 - t * rows_of)
        ends.append(jnp.where(lane % 2 == 0, from_east, -from_west) * across)

    held = [ends_ref[t] for t in range(parts)]
    tiles = []
    for f in range(2):
        for i in sides:
            edge = 0.0
            if i == cells - 1:
                edge = edge + weight(cells) * lat_in[1, f]
            if i == 0:
                edge = edge - weight(-1) * lat_in[0, f]
            tile = x_ref[f * cells + i]
            tile = (tile - edge if f == 0 else tile + edge) * scale(i)
            x_ref[f * cells + i] = tile
            held = take_ends(tile, f, i, held)
            tiles.append(jnp.where(inside, tile, 0.0))
    tiles.append(jnp.concatenate([held[t] + ends[t] for t in range(parts)], axis=0))
    high, low = gram_pair(tiles, snaps)
    if middle:
        high, more = two_sum(high, inner_ref[0])
        high, low = two_sum(high, low + (more + inner_ref[1]))

    def whole_tile(f, i):
        at = f * cells + i
        tile = x_ref[at]
        edge = jnp.concatenate([roll(ends[t], -2 * at - 1) for t in range(parts)], axis=0)
        return jnp.where(inside, tile, tile + edge)

    pending = []

    def exchange(buf, slot, count, target, at, parts):
        rows = 0
        for part in parts:
            buf[slot, pl.ds(rows, part.shape[0])] = part
            rows += part.shape[0]
        for d in peer_order(count):
            copy = pltpu.make_async_remote_copy(
                src_ref=buf.at[slot],
                dst_ref=buf.at[slot],
                send_sem=sum_send.at[at],
                recv_sem=sum_recv.at[at],
                device_id=target(shifted(slot, d, count)),
                device_id_type=pl.DeviceIdType.LOGICAL,
            )
            copy.start()
        if at == 0:
            for f in range(2):
                for i in range(cells):
                    column = (f * cells + i) * width
                    for index, part in enumerate(three(whole_tile(f, i))):
                        x_parts[pl.ds(index * snaps, snaps), pl.ds(column, width)] = part
        arrived = buf.at[pl.ds(0, count - 1)]
        pending.append((arrived, sum_send.at[at]))
        pltpu.make_async_copy(arrived, arrived, sum_recv.at[at]).wait()
        edges = [buf[index, pl.ds(SUBS, 1)] for index in range(count)]
        while len(edges) > 1:
            edges = [sum(edges[at : at + 2]) for at in range(0, len(edges), 2)]
        zero = jnp.zeros((SUBS, LANES), jnp.float32)
        totals = []
        for index in range(count):
            error = buf[index, pl.ds(SUBS + 1, SUBS)] if len(parts) > 2 else zero
            totals.append((buf[index, pl.ds(0, SUBS)], error))
        while len(totals) > 1:
            merged = []
            for at in range(0, len(totals) - 1, 2):
                (a, b), (x, y) = totals[at], totals[at + 1]
                high, low = two_sum(a, x)
                merged.append((high, low + (b + y)))
            if len(totals) % 2:
                merged.append(totals[-1])
            totals = merged
        return totals[0][0], edges[0], totals[0][1]

    bundle = message(high, low, snaps)
    if len(sum_bufs) == 1:
        everyone = lat_size * lon_size
        bundle = exchange(sum_bufs[0], lat * lon_size + lon, everyone, lambda at: at, 0, bundle)
    else:
        bundle = exchange(sum_bufs[0], lon, lon_size, lambda at: lat * lon_size + at, 0, bundle)
        bundle = exchange(sum_bufs[1], lat, lat_size, lambda at: at * lon_size + lon, 1, bundle)
    local, edge, error = bundle
    ahead = place(snaps)
    total, error = two_sum(local, error)
    total = jnp.where(ahead > 0, total + error, total)
    error = jnp.where(ahead > 0, 0.0, error)

    groups = snaps // SUBS
    sub = iota((SUBS, LANES), 0)
    high, low = restore(total, error, edge, snaps)
    first, lower = factorize(
        lambda g, k: total[:, g * snaps + k : g * snaps + k + 1],
        [high[g * SUBS : (g + 1) * SUBS] for g in range(groups)],
        snaps,
    )
    inverse = first[:, :snaps]
    hold_ref[0] = first
    gap = residual(high, low, lower, snaps)
    moved = pair_dot(gap, inverse, ((1,), (1,)))
    moved = pair_dot(inverse, moved, ((1,), (0,)))
    start = []
    for g in range(groups):
        at = iota((SUBS, snaps), 0) + g * SUBS
        unit = jnp.where(iota((SUBS, snaps), 1) == at, 1.0, 0.0)
        start.append(moved[g * SUBS : (g + 1) * SUBS] + unit)
    hold_ref[1, :, :snaps] = moved

    for at, copy in enumerate(copies):
        if at == 0:
            pl.when(lat < lat_size - 1)(copy.wait_send)
        elif at == 1:
            pl.when(lat > 0)(copy.wait_send)
        else:
            copy.wait_send()
    for sent, send in pending:
        pltpu.make_async_copy(sent, sent, send).wait()

    w = [part.astype(jnp.float32) for part in three(hold_ref[0])]
    quarters = LANES // snaps
    terms = [(0, 0), (0, 1), (0, 2), (1, 0), (1, 1), (2, 0)]
    left = []
    for at in range(0, len(terms), quarters):
        tiles = [
            pltpu.roll(w[a], index * snaps, 1) if index else w[a]
            for index, (a, b) in enumerate(terms[at : at + quarters])
        ]
        left.append(sum(tiles[1:], tiles[0]).astype(jnp.bfloat16))
    left = jnp.concatenate(left, axis=1)[:, : len(terms) * snaps]
    for at in range(0, 2 * cells * width, 2 * width):
        x = [x_parts[b * snaps : (b + 1) * snaps, at : at + 2 * width] for b in range(3)]
        right = jnp.concatenate([x[b] for a, b in terms], axis=0)
        solved_ref[:, at : at + 2 * width] = lax.dot_general(
            left, right, (((1,), (0,)), ((), ())), preferred_element_type=jnp.float32
        )
    second, lower_two = factorize(lambda g, k: start[g][:, k : k + 1], start, snaps)
    turn_ref[...] = second * root
    factor_ref[0] = lower
    factor_ref[1] = lower_two


def shifted(me, d, count):
    if count & (count - 1) == 0:
        return me ^ d
    return (me + d) % count


def peer_order(count):
    return sorted(range(1, count), key=lambda d: (-((d >> 1) & 3), -(d >> 3), d))


def finish(root, solved_ref, turn_ref, lower_ref, modes_hbm, factor_hbm, modes_ref, flat_ref, sem):
    snaps, _, cells, width = modes_hbm.shape
    bulk, rest = two(turn_ref[...][:, :snaps])
    stores = []

    def one(m, n):
        return lax.dot_general(
            m, n, (((1,), (0,)), ((), ())), preferred_element_type=jnp.float32
        )

    for f in range(2):
        for i in range(0, cells, 2):
            at = (f * cells + i) * width
            main, tail = two(solved_ref[:, at : at + 2 * width])
            modes = one(bulk, main) + (one(bulk, tail) + one(rest, main))
            for c in range(2):
                modes_ref[f, i + c] = modes[:, c * width : (c + 1) * width]
                stores.append(
                    pltpu.make_async_copy(modes_ref.at[f, i + c], modes_hbm.at[:, f, i + c], sem)
                )
                stores[-1].start()
    lower, lower_two = lower_ref[0], lower_ref[1]
    shape = (snaps, LANES)
    lower_two = pltpu.roll(lower_two, LANES - snaps, 1)
    wide = jnp.concatenate([jnp.zeros((snaps, LANES), jnp.float32), lower_two], axis=0)
    flat = dot(lower[:, : 2 * snaps], wide, ((1,), (0,))) / root
    flat_ref[...] = jnp.transpose(flat)[:snaps, :snaps]
    stores.append(pltpu.make_async_copy(flat_ref, factor_hbm, sem))
    stores[-1].start()
    for store in stores:
        store.wait()


def shards(sizes, wind_u, wind_v):
    snaps, cells, width = wind_u.shape
    lat_size, lon_size, cores = sizes
    chips = lat_size * lon_size // cores
    f32 = jnp.float32
    dma = pltpu.SemaphoreType.DMA
    vmem = pl.BlockSpec(memory_space=pltpu.VMEM)
    hbm = pl.BlockSpec(memory_space=pltpu.HBM)
    root = math.sqrt(2 * lat_size * cells * lon_size * width)
    if lat_size * lon_size <= DIRECT:
        sum_bufs = [pltpu.VMEM((lat_size * lon_size, SUBS + 1, LANES), f32)]
    else:
        sum_bufs = [
            pltpu.VMEM((lon_size, SUBS + 1, LANES), f32),
            pltpu.VMEM((lat_size, 2 * SUBS + 1, LANES), f32),
        ]
    held = pl.pallas_call(
        functools.partial(kernel, sizes, root),
        out_shape=(
            pltpu.VMEM((snaps, 2 * cells * width), f32),
            pltpu.VMEM((snaps, LANES), f32),
            pltpu.VMEM((2, snaps, LANES), f32),
        ),
        in_specs=[hbm, hbm],
        out_specs=(vmem, vmem, vmem),
        scratch_shapes=[
            pltpu.VMEM((2, cells, snaps, width), f32),
            pltpu.VMEM((2 * cells, snaps, width), f32),
            pltpu.VMEM((2, snaps, LANES), f32),
            pltpu.VMEM((snaps // SUBS, SUBS, LANES), f32),
            pltpu.VMEM((2, SUBS, LANES), f32),
            pltpu.VMEM((2, 2, snaps, width), f32),
            pltpu.VMEM((SUBS, LANES), f32),
            pltpu.VMEM((2, SUBS, LANES), f32),
            pltpu.VMEM((3 * snaps, 2 * cells * width), jnp.bfloat16),
            sum_bufs,
            dma((2,)),
            dma((2,)),
            dma((2,)),
            dma((2,)),
            dma((len(sum_bufs),)),
            dma((len(sum_bufs),)),
            pltpu.SemaphoreType.REGULAR,
            pltpu.SemaphoreType.REGULAR,
            dma,
        ],
        compiler_params=pltpu.CompilerParams(
            collective_id=0, has_side_effects=True, vmem_limit_bytes=VMEM_BYTES
        ),
    )(*(pltpu.with_memory_space_constraint(w, pltpu.HBM) for w in (wind_u, wind_v)))
    anywhere = pl.BlockSpec(memory_space=pl.ANY)
    return pl.pallas_call(
        functools.partial(finish, root),
        out_shape=(
            jax.ShapeDtypeStruct((snaps, 2, cells, width), f32),
            jax.ShapeDtypeStruct((snaps, snaps), f32),
        ),
        in_specs=[vmem, vmem, vmem],
        out_specs=(anywhere, anywhere),
        scratch_shapes=[
            pltpu.VMEM((2, cells, snaps, width), f32),
            pltpu.VMEM((snaps, snaps), f32),
            dma,
        ],
        compiler_params=pltpu.CompilerParams(vmem_limit_bytes=VMEM_BYTES),
    )(*held)


def solution(mesh):
    lat_size, lon_size = mesh.shape["lat"], mesh.shape["lon"]
    sizes = (lat_size, lon_size, 2 if lon_size % 2 == 0 else 1)
    in_specs = (P(None, "lat", "lon"), P(None, "lat", "lon"))
    out_specs = (P(None, None, "lat", "lon"), P())
    return jax.shard_map(
        functools.partial(shards, sizes),
        mesh=mesh,
        in_specs=in_specs,
        out_specs=out_specs,
        check_vma=False,
    )
```

```python
import functools
import math

import jax
import jax.numpy as jnp
from jax import lax
from jax.experimental import pallas as pl
from jax.experimental.pallas import tpu as pltpu
from jax.sharding import PartitionSpec as P

MESH = pl.DeviceIdType.MESH
LANES = 128
SUBS = 8
DIRECT = 64
VMEM_BYTES = 8 * 1024 * 1024


def iota(shape, dim):
    return lax.broadcasted_iota(jnp.int32, shape, dim)


def dot(left, right, dims):
    return lax.dot_general(
        left,
        right,
        (dims, ((), ())),
        precision=lax.Precision.HIGHEST,
        preferred_element_type=jnp.float32,
    )


def two(tile):
    high = tile.astype(jnp.bfloat16)
    return high, (tile - high.astype(jnp.float32)).astype(jnp.bfloat16)


def three(tile):
    high = tile.astype(jnp.bfloat16)
    tile = tile - high.astype(jnp.float32)
    return (high,) + two(tile)


def pair_dot(left, right, dims):
    a, b = two(left)
    x, y = two(right)

    def one(m, n):
        return lax.dot_general(m, n, (dims, ((), ())), preferred_element_type=jnp.float32)

    return one(a, x) + (one(a, y) + one(b, x))


def roll(tile, shift):
    shift = shift % LANES
    return tile if shift == 0 else pltpu.roll(tile, shift, 1)


def spread(tile):
    return jnp.broadcast_to(tile, (SUBS, LANES))


def two_sum(a, b):
    total = a + b
    part = total - a
    return total, (a - (total - part)) + (b - part)


def power_above(bound):
    wide = bound * (2.0**23 + 1.0)
    return 2.0 * jnp.abs(wide - wide * (1.0 - 2.0**-24))


def fixed_slices(tile, unit, bits):
    out = []
    for count in bits:
        magic = unit * (1.5 * 2.0 ** (23 - count))
        part = (tile + magic) - magic
        out.append(part.astype(jnp.bfloat16))
        tile = tile - part
    out.append(tile.astype(jnp.bfloat16))
    return out


def factorize(source, upper, n):
    groups = n // SUBS
    lane = iota((SUBS, LANES), 1)
    sub = iota((SUBS, LANES), 0)
    columns = {}

    def bring(first, last, take):
        for k in range(first * SUBS, min(last, groups) * SUBS):
            for g in range(k // SUBS, groups):
                columns[g, k] = spread(take(g, k))

    bring(0, 2, source)
    upper = list(upper)
    rows = [jnp.where(lane == sub + g * SUBS, 1.0, 0.0) for g in range(groups)]
    pivots = [None] * groups
    lower = [jnp.zeros((SUBS, LANES), jnp.float32)] * groups
    across = jnp.ones((SUBS, LANES), jnp.float32)
    for k in range(n):
        r, s = divmod(k, SUBS)
        if s == 0 and r > 0:
            bring(r + 1, r + 2, lambda g, j: upper[g][:, j : j + 1])
        pivot = spread(columns[r, k][s : s + 1, :])
        pivots[r] = pivot if s == 0 else jnp.where(sub == s, pivot, pivots[r])
        across = jnp.where(lane == n + k, pivot, across)
        inverse = 1.0 / pivot
        scaled = {g: columns[g, k] * inverse for g in range(r, groups)}
        for j in range(k + 1, min(n, (r + 2) * SUBS)):
            head = spread(columns[j // SUBS, k][j % SUBS : j % SUBS + 1, :])
            for g in range(j // SUBS, groups):
                columns[g, j] = columns[g, j] - scaled[g] * head
        pivot_row = spread(rows[r][s : s + 1, :])
        upper_row = jnp.broadcast_to(upper[r][s : s + 1, :], upper[r].shape)
        for g in range(r, groups):
            lower[g] = jnp.where(lane == n + k, columns[g, k], lower[g])
            factor = scaled[g]
            if g == r:
                if s == SUBS - 1:
                    continue
                factor = jnp.where(sub > s, factor, 0.0)
            rows[g] = rows[g] - factor * pivot_row
            if r + 2 < groups:
                upper[g] = upper[g] - factor[:, : upper_row.shape[1]] * upper_row
    across = 1.0 / jnp.sqrt(across)
    out, left = [], []
    for g in range(groups):
        out.append(rows[g] * (1.0 / jnp.sqrt(pivots[g])))
        keep = (lane >= n) & (lane - n - g * SUBS <= sub)
        left.append(jnp.where(keep, lower[g] * across, 0.0))
    return jnp.concatenate(out, axis=0), jnp.concatenate(left, axis=0)


def gram_pair(tiles, n):
    groups = n // SUBS
    peak = jnp.max(functools.reduce(jnp.maximum, map(jnp.abs, tiles)), axis=1, keepdims=True)
    unit = power_above(jnp.broadcast_to(peak, (n, LANES)))
    pieces = [fixed_slices(tile, unit, (5, 12, 19)) for tile in tiles]
    stack = jnp.concatenate(
        [jnp.concatenate([piece[a] for piece in pieces], axis=1) for a in range(4)], axis=0
    )
    gram = lax.dot_general(
        stack, stack, (((1,), (1,)), ((), ())), preferred_element_type=jnp.float32
    )
    quarter = iota((SUBS, LANES), 1) // n

    def part(a, b):
        total = None
        for g in range(groups):
            at = a * n + g * SUBS
            moved = roll(gram[at : at + SUBS], n * (g - b))
            total = moved if total is None else jnp.where(quarter == g, moved, total)
        return total

    def term(a, b):
        return part(a, b) if a == b else part(a, b) + part(b, a)

    high, low = two_sum(term(0, 0), term(0, 1))
    high, more = two_sum(high, term(0, 2) + term(1, 1))
    tiny = (term(1, 3) + term(2, 2)) + (term(2, 3) + term(3, 3))
    return two_sum(high, (low + more) + ((term(0, 3) + term(1, 2)) + tiny))


def message(high, low, n):
    ahead = place(n)
    edge = jnp.sum(jnp.where(ahead == 0, low, 0.0), axis=0, keepdims=True)
    return jnp.where(ahead > 0, low, high), edge


def place(n):
    lane = iota((SUBS, LANES), 1)
    return lane % n - (lane // n * SUBS + iota((SUBS, LANES), 0))


def restore(total, error, edge, n):
    groups = n // SUBS
    shape = (n, n)
    row, col = iota(shape, 0), iota(shape, 1)

    def unpack(packed):
        return jnp.concatenate([roll(packed, -g * n) for g in range(groups)], axis=0)

    def flip(tile):
        return jnp.transpose(tile)[:n]

    whole, rest = unpack(total), unpack(error)
    whole_flip, rest_flip = flip(whole)[:, :n], flip(rest)[:, :n]
    whole, rest = whole[:, :n], rest[:, :n]
    diagonal = jnp.zeros((1, LANES), jnp.float32)
    lane = iota((1, LANES), 1)
    for g in range(groups):
        diagonal = jnp.where(lane // SUBS == g, roll(edge, -g * n), diagonal)
    diagonal = jnp.broadcast_to(diagonal[:, :n], shape)
    high = jnp.where(row >= col, whole, whole_flip)
    low = jnp.where(row > col, rest + whole_flip, rest_flip + whole)
    return high, jnp.where(row == col, rest + diagonal, low)


def residual(high, low, lower, n):
    row, col = iota((n, n), 0), iota((n, n), 1)
    peak = jnp.sqrt(jnp.sum(jnp.where(row == col, high, 0.0), axis=1, keepdims=True)) * 1.01
    unit = power_above(jnp.broadcast_to(peak, (n, LANES)))
    slices = fixed_slices(lower, unit, (8, 17, 26))
    stack = jnp.concatenate(slices, axis=0)
    products = [
        lax.dot_general(
            stack[:, : 2 * n],
            one[:, : 2 * n],
            (((1,), (1,)), ((), ())),
            preferred_element_type=jnp.float32,
        )
        for one in slices
    ]

    def order(count):
        total = None
        for a in range(4):
            b = count - a
            if 0 <= b < 4:
                one = products[b][a * n : (a + 1) * n]
                total = one if total is None else total + one
        return total

    first, low_one = two_sum(high, -order(0))
    first, low_two = two_sum(first, -order(1))
    first, low_three = two_sum(first, -order(2))
    tail = (low_one + low_two) + (low_three + (low - (order(3) + (order(4) + order(5)))))
    return first + tail


def kernel(
    sizes,
    root,
    u_hbm,
    v_hbm,
    solved_ref,
    turn_ref,
    factor_ref,
    wind_ref,
    x_ref,
    hold_ref,
    ends_ref,
    inner_ref,
    lat_in,
    lon_out,
    lon_in,
    x_parts,
    sum_bufs,
    lat_send,
    lat_recv,
    lon_send,
    lon_recv,
    sum_send,
    sum_recv,
    up_sem,
    down_sem,
    local_sem,
):
    lat_size, lon_size, cores = sizes
    _, cells, snaps, width = wind_ref.shape
    depth = lon_size // cores
    chips = lat_size * depth
    lat = lax.axis_index("lat")
    lon = lax.axis_index("lon")
    z = lon // cores
    core = lon % cores
    mine = lat * depth + z
    lat_up = (lat + 1) % lat_size
    lat_down = (lat + lat_size - 1) % lat_size
    east = (lon + 1) % lon_size
    west = (lon + lon_size - 1) % lon_size

    barrier = pltpu.get_barrier_semaphore()

    first_z, last_z = z == 0, z == depth - 1
    below, above = lon - cores, lon + cores
    ring = [(lat, east), (lat, west)]
    if cores == 2:
        ring = [(lat, (lon + lon_size + 2 * core - 1) % lon_size)]
    around = [
        ((lat + a) % lat_size, z * cores + (core + b) % cores)
        for a in range(lat_size)
        for b in range(cores)
        if a or b
    ]

    def greet(peer):
        pl.semaphore_signal(barrier, inc=1, device_id=peer, device_id_type=MESH)

    for peer in ring + around:
        greet(peer)
    pl.when(jnp.logical_not(first_z))(lambda: greet((lat, below)))
    pl.when(jnp.logical_not(last_z))(lambda: greet((lat, above)))
    callers = len(ring + around) + jnp.where(first_z, 0, 1) + jnp.where(last_z, 0, 1)

    loads = [
        pltpu.make_async_copy(hbm.at[:, i], wind_ref.at[f, i], local_sem)
        for f, hbm in enumerate((u_hbm, v_hbm))
        for i in range(cells)
    ]
    for load in loads:
        load.start()

    pltpu.make_async_copy(wind_ref, wind_ref, local_sem).wait()

    lane = iota((SUBS, LANES), 1)
    parts = snaps // SUBS
    winds = [[wind_ref[f, i] for i in range(cells)] for f in range(2)]
    edges = [jnp.zeros((SUBS, LANES), jnp.float32)] * parts
    for f in range(2):
        for i in range(cells):
            for t in range(parts):
                q = (t * 2 + 1 - f) * cells + i
                tile = winds[f][i][t * SUBS : (t + 1) * SUBS]
                edges[t] = jnp.where(lane // 2 == q, roll(tile, 2 * q + 1), edges[t])
    while len(edges) > 1:
        edges = [sum(edges[at : at + 2]) for at in range(0, len(edges), 2)]
    lon_out[...] = edges[0]

    pl.semaphore_wait(barrier, callers)

    copies = []
    for way, target in ((0, lat_up), (1, lat_down)):
        copies.append(
            pltpu.make_async_remote_copy(
                src_ref=wind_ref.at[:, 0 if way else cells - 1],
                dst_ref=lat_in.at[way],
                send_sem=lat_send.at[way],
                recv_sem=lat_recv.at[way],
                device_id=(target, lon),
                device_id_type=MESH,
            )
        )
    for way, target in ((0, east), (1, west)):
        copies.append(
            pltpu.make_async_remote_copy(
                src_ref=lon_out,
                dst_ref=lon_in.at[way],
                send_sem=lon_send.at[way],
                recv_sem=lon_recv.at[way],
                device_id=(lat, target),
                device_id_type=MESH,
            )
        )
    for copy in copies[2:]:
        copy.start()
    pl.when(lat < lat_size - 1)(copies[0].start)
    pl.when(lat > 0)(copies[1].start)

    upper_core, lower_core = core == cores - 1, core == 0

    def tell(sem, targets):
        for target in targets:
            pl.semaphore_signal(sem, inc=1, device_id=(lat, target), device_id_type=MESH)

    def ascend():
        tell(up_sem, [above, east] if cores > 1 else [above])

    def descend():
        tell(down_sem, [below, west] if cores > 1 else [below])

    if depth > 1:
        pl.when(jnp.logical_and(first_z, upper_core))(ascend)
        pl.when(jnp.logical_and(last_z, lower_core))(descend)

    nlat = lat_size * cells
    step = 2.0 * math.pi / (lon_size * width)
    row_index = lat * cells - 1 + iota((2 * SUBS, LANES), 0)
    cosines = jnp.cos((row_index.astype(jnp.float32) + 0.5 - nlat / 2) * step)
    weights = jnp.where((row_index >= 0) & (row_index < nlat), cosines, 0.0)
    scales = 0.5 / jnp.sqrt(cosines)

    def weight(i):
        return weights[i + 1 : i + 2, :]

    def scale(i):
        return scales[i + 1 : i + 2, :]

    wide = iota((snaps, LANES), 1)

    def lon_inner(tile):
        right = jnp.where(wide == LANES - 1, 0.0, pltpu.roll(tile, LANES - 1, 1))
        return right - jnp.where(wide == 0, 0.0, pltpu.roll(tile, 1, 1))

    def lat_inner(f, i):
        high = weight(i + 1) * winds[f][i + 1] if i + 1 < cells else 0.0
        low = weight(i - 1) * winds[f][i - 1] if i > 0 else 0.0
        return high - low

    def inner(f, i):
        if f == 0:
            return lon_inner(winds[1][i]) - lat_inner(0, i)
        return lon_inner(winds[0][i]) + lat_inner(1, i)

    sides = sorted({0, cells - 1})
    middle = [i for i in range(cells) if i not in sides]
    inside = (wide > 0) & (wide < LANES - 1)
    rows_of = 2 * 2 * cells

    def take_ends(tile, f, i, held):
        at = f * cells + i
        out = []
        for t in range(parts):
            moved = roll(tile[t * SUBS : (t + 1) * SUBS], 2 * at + 1)
            out.append(held[t] + jnp.where(lane // 2 == at, moved, 0.0))
        return out

    held = [jnp.zeros((SUBS, LANES), jnp.float32)] * parts
    tiles = []
    for f in range(2):
        for i in middle:
            tile = inner(f, i) * scale(i)
            x_ref[f * cells + i] = tile
            held = take_ends(tile, f, i, held)
            tiles.append(jnp.where(inside, tile, 0.0))
        for i in sides:
            x_ref[f * cells + i] = inner(f, i)
    for t in range(parts):
        ends_ref[t] = held[t]
    if middle:
        high, low = gram_pair(tiles, snaps)
        inner_ref[0] = high
        inner_ref[1] = low

    if depth > 1:
        @pl.when(jnp.logical_not(first_z))
        def _():
            pl.semaphore_wait(up_sem, 1)
            pl.when(jnp.logical_and(upper_core, jnp.logical_not(last_z)))(ascend)

        @pl.when(jnp.logical_not(last_z))
        def _():
            pl.semaphore_wait(down_sem, 1)
            pl.when(jnp.logical_and(lower_core, jnp.logical_not(first_z)))(descend)

    for at, copy in enumerate(copies):
        if at == 0:
            pl.when(lat > 0)(copy.wait_recv)
        elif at == 1:
            pl.when(lat < lat_size - 1)(copy.wait_recv)
        else:
            copy.wait_recv()

    across = jnp.zeros((SUBS, LANES), jnp.float32)
    for i in range(cells):
        across = jnp.where(lane // 2 % cells == i, scale(i), across)
    across = jnp.where(lane < rows_of, across, 0.0)
    ends = []
    for t in range(parts):
        from_east = roll(lon_in[1], -1 - t * rows_of)
        from_west = roll(lon_in[0], 1 - t * rows_of)
        ends.append(jnp.where(lane % 2 == 0, from_east, -from_west) * across)

    held = [ends_ref[t] for t in range(parts)]
    tiles = []
    for f in range(2):
        for i in sides:
            edge = 0.0
            if i == cells - 1:
                edge = edge + weight(cells) * lat_in[1, f]
            if i == 0:
                edge = edge - weight(-1) * lat_in[0, f]
            tile = x_ref[f * cells + i]
            tile = (tile - edge if f == 0 else tile + edge) * scale(i)
            x_ref[f * cells + i] = tile
            held = take_ends(tile, f, i, held)
            tiles.append(jnp.where(inside, tile, 0.0))
    tiles.append(jnp.concatenate([held[t] + ends[t] for t in range(parts)], axis=0))
    high, low = gram_pair(tiles, snaps)
    if middle:
        high, more = two_sum(high, inner_ref[0])
        high, low = two_sum(high, low + (more + inner_ref[1]))

    def whole_tile(f, i):
        at = f * cells + i
        tile = x_ref[at]
        edge = jnp.concatenate([roll(ends[t], -2 * at - 1) for t in range(parts)], axis=0)
        return jnp.where(inside, tile, tile + edge)

    pending = []

    def exchange(buf, slot, count, target, at, parts):
        rows = 0
        for part in parts:
            buf[slot, pl.ds(rows, part.shape[0])] = part
            rows += part.shape[0]
        for d in peer_order(count):
            copy = pltpu.make_async_remote_copy(
                src_ref=buf.at[slot],
                dst_ref=buf.at[slot],
                send_sem=sum_send.at[at],
                recv_sem=sum_recv.at[at],
                device_id=target(shifted(slot, d, count)),
                device_id_type=pl.DeviceIdType.LOGICAL,
            )
            copy.start()
        if at == 0:
            for f in range(2):
                for i in range(cells):
                    column = (f * cells + i) * width
                    for index, part in enumerate(three(whole_tile(f, i))):
                        x_parts[pl.ds(index * snaps, snaps), pl.ds(column, width)] = part
        arrived = buf.at[pl.ds(0, count - 1)]
        pending.append((arrived, sum_send.at[at]))
        pltpu.make_async_copy(arrived, arrived, sum_recv.at[at]).wait()
        edges = [buf[index, pl.ds(SUBS, 1)] for index in range(count)]
        while len(edges) > 1:
            edges = [sum(edges[at : at + 2]) for at in range(0, len(edges), 2)]
        zero = jnp.zeros((SUBS, LANES), jnp.float32)
        totals = []
        for index in range(count):
            error = buf[index, pl.ds(SUBS + 1, SUBS)] if len(parts) > 2 else zero
            totals.append((buf[index, pl.ds(0, SUBS)], error))
        while len(totals) > 1:
            merged = []
            for at in range(0, len(totals) - 1, 2):
                (a, b), (x, y) = totals[at], totals[at + 1]
                high, low = two_sum(a, x)
                merged.append((high, low + (b + y)))
            if len(totals) % 2:
                merged.append(totals[-1])
            totals = merged
        return totals[0][0], edges[0], totals[0][1]

    bundle = message(high, low, snaps)
    if len(sum_bufs) == 1:
        everyone = lat_size * lon_size
        bundle = exchange(sum_bufs[0], lat * lon_size + lon, everyone, lambda at: at, 0, bundle)
    else:
        bundle = exchange(sum_bufs[0], lon, lon_size, lambda at: lat * lon_size + at, 0, bundle)
        bundle = exchange(sum_bufs[1], lat, lat_size, lambda at: at * lon_size + lon, 1, bundle)
    local, edge, error = bundle
    ahead = place(snaps)
    total, error = two_sum(local, error)
    total = jnp.where(ahead > 0, total + error, total)
    error = jnp.where(ahead > 0, 0.0, error)

    groups = snaps // SUBS
    sub = iota((SUBS, LANES), 0)
    high, low = restore(total, error, edge, snaps)
    first, lower = factorize(
        lambda g, k: total[:, g * snaps + k : g * snaps + k + 1],
        [high[g * SUBS : (g + 1) * SUBS] for g in range(groups)],
        snaps,
    )
    inverse = first[:, :snaps]
    hold_ref[0] = first
    gap = residual(high, low, lower, snaps)
    moved = pair_dot(gap, inverse, ((1,), (1,)))
    moved = pair_dot(inverse, moved, ((1,), (0,)))
    start = []
    for g in range(groups):
        at = iota((SUBS, snaps), 0) + g * SUBS
        unit = jnp.where(iota((SUBS, snaps), 1) == at, 1.0, 0.0)
        start.append(moved[g * SUBS : (g + 1) * SUBS] + unit)
    hold_ref[1, :, :snaps] = moved

    for at, copy in enumerate(copies):
        if at == 0:
            pl.when(lat < lat_size - 1)(copy.wait_send)
        elif at == 1:
            pl.when(lat > 0)(copy.wait_send)
        else:
            copy.wait_send()
    for sent, send in pending:
        pltpu.make_async_copy(sent, sent, send).wait()

    w = [part.astype(jnp.float32) for part in three(hold_ref[0])]
    quarters = LANES // snaps
    terms = [(0, 0), (0, 1), (0, 2), (1, 0), (1, 1), (2, 0)]
    left = []
    for at in range(0, len(terms), quarters):
        tiles = [
            pltpu.roll(w[a], index * snaps, 1) if index else w[a]
            for index, (a, b) in enumerate(terms[at : at + quarters])
        ]
        left.append(sum(tiles[1:], tiles[0]).astype(jnp.bfloat16))
    left = jnp.concatenate(left, axis=1)[:, : len(terms) * snaps]
    for at in range(0, 2 * cells * width, 2 * width):
        x = [x_parts[b * snaps : (b + 1) * snaps, at : at + 2 * width] for b in range(3)]
        right = jnp.concatenate([x[b] for a, b in terms], axis=0)
        solved_ref[:, at : at + 2 * width] = lax.dot_general(
            left, right, (((1,), (0,)), ((), ())), preferred_element_type=jnp.float32
        )
    second, lower_two = factorize(lambda g, k: start[g][:, k : k + 1], start, snaps)
    turn_ref[...] = second * root
    factor_ref[0] = lower
    factor_ref[1] = lower_two


def shifted(me, d, count):
    if count & (count - 1) == 0:
        return me ^ d
    return (me + d) % count


def peer_order(count):
    return sorted(range(1, count), key=lambda d: (-((d >> 1) & 3), -(d >> 3), d))


def finish(root, solved_ref, turn_ref, lower_ref, modes_hbm, factor_hbm, modes_ref, flat_ref, sem):
    snaps, _, cells, width = modes_hbm.shape
    bulk, rest = two(turn_ref[...][:, :snaps])
    stores = []

    def one(m, n):
        return lax.dot_general(
            m, n, (((1,), (0,)), ((), ())), preferred_element_type=jnp.float32
        )

    for f in range(2):
        for i in range(0, cells, 2):
            at = (f * cells + i) * width
            main, tail = two(solved_ref[:, at : at + 2 * width])
            modes = one(bulk, main) + (one(bulk, tail) + one(rest, main))
            for c in range(2):
                modes_ref[f, i + c] = modes[:, c * width : (c + 1) * width]
                stores.append(
                    pltpu.make_async_copy(modes_ref.at[f, i + c], modes_hbm.at[:, f, i + c], sem)
                )
                stores[-1].start()
    lower, lower_two = lower_ref[0], lower_ref[1]
    shape = (snaps, LANES)
    lower_two = pltpu.roll(lower_two, LANES - snaps, 1)
    wide = jnp.concatenate([jnp.zeros((snaps, LANES), jnp.float32), lower_two], axis=0)
    flat = dot(lower[:, : 2 * snaps], wide, ((1,), (0,))) / root
    flat_ref[...] = jnp.transpose(flat)[:snaps, :snaps]
    stores.append(pltpu.make_async_copy(flat_ref, factor_hbm, sem))
    stores[-1].start()
    for store in stores:
        store.wait()


def shards(sizes, wind_u, wind_v):
    snaps, cells, width = wind_u.shape
    lat_size, lon_size, cores = sizes
    chips = lat_size * lon_size // cores
    f32 = jnp.float32
    dma = pltpu.SemaphoreType.DMA
    vmem = pl.BlockSpec(memory_space=pltpu.VMEM)
    hbm = pl.BlockSpec(memory_space=pltpu.HBM)
    root = math.sqrt(2 * lat_size * cells * lon_size * width)
    if lat_size * lon_size <= DIRECT:
        sum_bufs = [pltpu.VMEM((lat_size * lon_size, SUBS + 1, LANES), f32)]
    else:
        sum_bufs = [
            pltpu.VMEM((lon_size, SUBS + 1, LANES), f32),
            pltpu.VMEM((lat_size, 2 * SUBS + 1, LANES), f32),
        ]
    held = pl.pallas_call(
        functools.partial(kernel, sizes, root),
        out_shape=(
            pltpu.VMEM((snaps, 2 * cells * width), f32),
            pltpu.VMEM((snaps, LANES), f32),
            pltpu.VMEM((2, snaps, LANES), f32),
        ),
        in_specs=[hbm, hbm],
        out_specs=(vmem, vmem, vmem),
        scratch_shapes=[
            pltpu.VMEM((2, cells, snaps, width), f32),
            pltpu.VMEM((2 * cells, snaps, width), f32),
            pltpu.VMEM((2, snaps, LANES), f32),
            pltpu.VMEM((snaps // SUBS, SUBS, LANES), f32),
            pltpu.VMEM((2, SUBS, LANES), f32),
            pltpu.VMEM((2, 2, snaps, width), f32),
            pltpu.VMEM((SUBS, LANES), f32),
            pltpu.VMEM((2, SUBS, LANES), f32),
            pltpu.VMEM((3 * snaps, 2 * cells * width), jnp.bfloat16),
            sum_bufs,
            dma((2,)),
            dma((2,)),
            dma((2,)),
            dma((2,)),
            dma((len(sum_bufs),)),
            dma((len(sum_bufs),)),
            pltpu.SemaphoreType.REGULAR,
            pltpu.SemaphoreType.REGULAR,
            dma,
        ],
        compiler_params=pltpu.CompilerParams(
            collective_id=0, has_side_effects=True, vmem_limit_bytes=VMEM_BYTES
        ),
    )(*(pltpu.with_memory_space_constraint(w, pltpu.HBM) for w in (wind_u, wind_v)))
    anywhere = pl.BlockSpec(memory_space=pl.ANY)
    return pl.pallas_call(
        functools.partial(finish, root),
        out_shape=(
            jax.ShapeDtypeStruct((snaps, 2, cells, width), f32),
            jax.ShapeDtypeStruct((snaps, snaps), f32),
        ),
        in_specs=[vmem, vmem, vmem],
        out_specs=(anywhere, anywhere),
        scratch_shapes=[
            pltpu.VMEM((2, cells, snaps, width), f32),
            pltpu.VMEM((snaps, snaps), f32),
            dma,
        ],
        compiler_params=pltpu.CompilerParams(vmem_limit_bytes=VMEM_BYTES),
    )(*held)


def solution(mesh):
    lat_size, lon_size = mesh.shape["lat"], mesh.shape["lon"]
    sizes = (lat_size, lon_size, 2 if lon_size % 2 == 0 else 1)
    in_specs = (P(None, "lat", "lon"), P(None, "lat", "lon"))
    out_specs = (P(None, None, "lat", "lon"), P())
    return jax.shard_map(
        functools.partial(shards, sizes),
        mesh=mesh,
        in_specs=in_specs,
        out_specs=out_specs,
        check_vma=False,
    )
```

```python
import functools
import math

import jax
import jax.numpy as jnp
from jax import lax
from jax.experimental import pallas as pl
from jax.experimental.pallas import tpu as pltpu
from jax.sharding import PartitionSpec as P

MESH = pl.DeviceIdType.MESH
LANES = 128
SUBS = 8
DIRECT = 64
VMEM_BYTES = 8 * 1024 * 1024


def iota(shape, dim):
    return lax.broadcasted_iota(jnp.int32, shape, dim)


def dot(left, right, dims):
    return lax.dot_general(
        left,
        right,
        (dims, ((), ())),
        precision=lax.Precision.HIGHEST,
        preferred_element_type=jnp.float32,
    )


def two(tile):
    high = tile.astype(jnp.bfloat16)
    return high, (tile - high.astype(jnp.float32)).astype(jnp.bfloat16)


def three(tile):
    high = tile.astype(jnp.bfloat16)
    tile = tile - high.astype(jnp.float32)
    return (high,) + two(tile)


def pair_dot(left, right, dims):
    a, b = two(left)
    x, y = two(right)

    def one(m, n):
        return lax.dot_general(m, n, (dims, ((), ())), preferred_element_type=jnp.float32)

    return one(a, x) + (one(a, y) + one(b, x))


def roll(tile, shift):
    shift = shift % LANES
    return tile if shift == 0 else pltpu.roll(tile, shift, 1)


def spread(tile):
    return jnp.broadcast_to(tile, (SUBS, LANES))


def two_sum(a, b):
    total = a + b
    part = total - a
    return total, (a - (total - part)) + (b - part)


def power_above(bound):
    wide = bound * (2.0**23 + 1.0)
    return 2.0 * jnp.abs(wide - wide * (1.0 - 2.0**-24))


def fixed_slices(tile, unit, bits):
    out = []
    for count in bits:
        magic = unit * (1.5 * 2.0 ** (23 - count))
        part = (tile + magic) - magic
        out.append(part.astype(jnp.bfloat16))
        tile = tile - part
    out.append(tile.astype(jnp.bfloat16))
    return out


def factorize(source, upper, n, base):
    groups = n // SUBS
    lane = iota((SUBS, LANES), 1)
    sub = iota((SUBS, LANES), 0)
    columns = {}

    def bring(first, last, take):
        for k in range(first * SUBS, min(last, groups) * SUBS):
            for g in range(k // SUBS, groups):
                columns[g, k] = spread(take(g, k))

    bring(0, 2, source)
    upper = list(upper)
    rows = [jnp.where(lane == sub + g * SUBS, 1.0, 0.0) for g in range(groups)]
    pivots = [None] * groups
    lower = [jnp.zeros((SUBS, LANES), jnp.float32)] * groups
    across = jnp.ones((SUBS, LANES), jnp.float32)
    for k in range(n):
        r, s = divmod(k, SUBS)
        if s == 0 and r > 0:
            bring(r + 1, r + 2, lambda g, j: upper[g][:, j : j + 1])
        pivot = spread(columns[r, k][s : s + 1, :])
        pivots[r] = pivot if s == 0 else jnp.where(sub == s, pivot, pivots[r])
        across = jnp.where(lane == base + k, pivot, across)
        inverse = 1.0 / pivot
        scaled = {g: columns[g, k] * inverse for g in range(r, groups)}
        for j in range(k + 1, min(n, (r + 2) * SUBS)):
            head = spread(columns[j // SUBS, k][j % SUBS : j % SUBS + 1, :])
            for g in range(j // SUBS, groups):
                columns[g, j] = columns[g, j] - scaled[g] * head
        pivot_row = spread(rows[r][s : s + 1, :])
        upper_row = jnp.broadcast_to(upper[r][s : s + 1, :], upper[r].shape)
        for g in range(r, groups):
            lower[g] = jnp.where(lane == base + k, columns[g, k], lower[g])
            factor = scaled[g]
            if g == r:
                if s == SUBS - 1:
                    continue
                factor = jnp.where(sub > s, factor, 0.0)
            rows[g] = rows[g] - factor * pivot_row
            if r + 2 < groups:
                upper[g] = upper[g] - factor[:, : upper_row.shape[1]] * upper_row
    across = 1.0 / jnp.sqrt(across)
    out, left = [], []
    for g in range(groups):
        out.append(rows[g] * (1.0 / jnp.sqrt(pivots[g])))
        keep = (lane >= base) & (lane - base - g * SUBS <= sub)
        left.append(jnp.where(keep, lower[g] * across, 0.0))
    return jnp.concatenate(out, axis=0), jnp.concatenate(left, axis=0)


def gram_pair(tiles, n):
    groups = n // SUBS
    peak = jnp.max(functools.reduce(jnp.maximum, map(jnp.abs, tiles)), axis=1, keepdims=True)
    unit = power_above(jnp.broadcast_to(peak, (n, LANES)))
    pieces = [fixed_slices(tile, unit, (5, 12, 19)) for tile in tiles]
    stack = jnp.concatenate(
        [jnp.concatenate([piece[a] for piece in pieces], axis=1) for a in range(4)], axis=0
    )
    gram = lax.dot_general(
        stack, stack, (((1,), (1,)), ((), ())), preferred_element_type=jnp.float32
    )
    quarter = iota((SUBS, LANES), 1) // n

    def part(a, b):
        total = None
        for g in range(groups):
            at = a * n + g * SUBS
            moved = roll(gram[at : at + SUBS], n * (g - b))
            total = moved if total is None else jnp.where(quarter == g, moved, total)
        return total

    def term(a, b):
        return part(a, b) if a == b else part(a, b) + part(b, a)

    high, low = two_sum(term(0, 0), term(0, 1))
    high, more = two_sum(high, term(0, 2) + term(1, 1))
    tiny = (term(1, 3) + term(2, 2)) + (term(2, 3) + term(3, 3))
    return two_sum(high, (low + more) + ((term(0, 3) + term(1, 2)) + tiny))


def message(high, low, n):
    ahead = place(n)
    edge = jnp.sum(jnp.where(ahead == 0, low, 0.0), axis=0, keepdims=True)
    return jnp.where(ahead > 0, low, high), edge


def place(n):
    lane = iota((SUBS, LANES), 1)
    return lane % n - (lane // n * SUBS + iota((SUBS, LANES), 0))


def restore(total, error, edge, n):
    groups = n // SUBS
    shape = (n, n)
    row, col = iota(shape, 0), iota(shape, 1)

    def unpack(packed):
        return jnp.concatenate([roll(packed, -g * n) for g in range(groups)], axis=0)

    def flip(tile):
        return jnp.transpose(tile)[:n]

    whole, rest = unpack(total), unpack(error)
    whole_flip, rest_flip = flip(whole)[:, :n], flip(rest)[:, :n]
    whole, rest = whole[:, :n], rest[:, :n]
    diagonal = jnp.zeros((1, LANES), jnp.float32)
    lane = iota((1, LANES), 1)
    for g in range(groups):
        diagonal = jnp.where(lane // SUBS == g, roll(edge, -g * n), diagonal)
    diagonal = jnp.broadcast_to(diagonal[:, :n], shape)
    high = jnp.where(row >= col, whole, whole_flip)
    low = jnp.where(row > col, rest + whole_flip, rest_flip + whole)
    return high, jnp.where(row == col, rest + diagonal, low)


def residual(high, low, lower, n):
    row, col = iota((n, n), 0), iota((n, n), 1)
    peak = jnp.sqrt(jnp.sum(jnp.where(row == col, high, 0.0), axis=1, keepdims=True)) * 1.01
    unit = power_above(jnp.broadcast_to(peak, (n, LANES)))
    slices = fixed_slices(lower, unit, (8, 17, 26))
    stack = jnp.concatenate(slices, axis=0)
    products = [
        lax.dot_general(
            stack[:, : 2 * n],
            one[:, : 2 * n],
            (((1,), (1,)), ((), ())),
            preferred_element_type=jnp.float32,
        )
        for one in slices
    ]

    def order(count):
        total = None
        for a in range(4):
            b = count - a
            if 0 <= b < 4:
                one = products[b][a * n : (a + 1) * n]
                total = one if total is None else total + one
        return total

    first, low_one = two_sum(high, -order(0))
    first, low_two = two_sum(first, -order(1))
    first, low_three = two_sum(first, -order(2))
    tail = (low_one + low_two) + (low_three + (low - (order(3) + (order(4) + order(5)))))
    return first + tail


def kernel(
    sizes,
    root,
    u_hbm,
    v_hbm,
    solved_ref,
    turn_ref,
    factor_ref,
    wind_ref,
    x_ref,
    hold_ref,
    ends_ref,
    inner_ref,
    lat_in,
    lon_out,
    lon_in,
    x_parts,
    sum_bufs,
    lat_send,
    lat_recv,
    lon_send,
    lon_recv,
    sum_send,
    sum_recv,
    up_sem,
    down_sem,
    local_sem,
):
    lat_size, lon_size, cores = sizes
    _, cells, snaps, width = wind_ref.shape
    depth = lon_size // cores
    chips = lat_size * depth
    lat = lax.axis_index("lat")
    lon = lax.axis_index("lon")
    z = lon // cores
    core = lon % cores
    mine = lat * depth + z
    lat_up = (lat + 1) % lat_size
    lat_down = (lat + lat_size - 1) % lat_size
    east = (lon + 1) % lon_size
    west = (lon + lon_size - 1) % lon_size

    barrier = pltpu.get_barrier_semaphore()

    first_z, last_z = z == 0, z == depth - 1
    below, above = lon - cores, lon + cores
    ring = [(lat, east), (lat, west)]
    if cores == 2:
        ring = [(lat, (lon + lon_size + 2 * core - 1) % lon_size)]
    around = [
        ((lat + a) % lat_size, z * cores + (core + b) % cores)
        for a in range(lat_size)
        for b in range(cores)
        if a or b
    ]

    def greet(peer):
        pl.semaphore_signal(barrier, inc=1, device_id=peer, device_id_type=MESH)

    for peer in ring + around:
        greet(peer)
    pl.when(jnp.logical_not(first_z))(lambda: greet((lat, below)))
    pl.when(jnp.logical_not(last_z))(lambda: greet((lat, above)))
    callers = len(ring + around) + jnp.where(first_z, 0, 1) + jnp.where(last_z, 0, 1)

    loads = [
        pltpu.make_async_copy(hbm.at[:, i], wind_ref.at[f, i], local_sem)
        for f, hbm in enumerate((u_hbm, v_hbm))
        for i in range(cells)
    ]
    for load in loads:
        load.start()

    pltpu.make_async_copy(wind_ref, wind_ref, local_sem).wait()

    lane = iota((SUBS, LANES), 1)
    parts = snaps // SUBS
    winds = [[wind_ref[f, i] for i in range(cells)] for f in range(2)]
    edges = [jnp.zeros((SUBS, LANES), jnp.float32)] * parts
    for f in range(2):
        for i in range(cells):
            for t in range(parts):
                q = (t * 2 + 1 - f) * cells + i
                tile = winds[f][i][t * SUBS : (t + 1) * SUBS]
                edges[t] = jnp.where(lane // 2 == q, roll(tile, 2 * q + 1), edges[t])
    while len(edges) > 1:
        edges = [sum(edges[at : at + 2]) for at in range(0, len(edges), 2)]
    lon_out[...] = edges[0]

    pl.semaphore_wait(barrier, callers)

    copies = []
    for way, target in ((0, lat_up), (1, lat_down)):
        copies.append(
            pltpu.make_async_remote_copy(
                src_ref=wind_ref.at[:, 0 if way else cells - 1],
                dst_ref=lat_in.at[way],
                send_sem=lat_send.at[way],
                recv_sem=lat_recv.at[way],
                device_id=(target, lon),
                device_id_type=MESH,
            )
        )
    for way, target in ((0, east), (1, west)):
        copies.append(
            pltpu.make_async_remote_copy(
                src_ref=lon_out,
                dst_ref=lon_in.at[way],
                send_sem=lon_send.at[way],
                recv_sem=lon_recv.at[way],
                device_id=(lat, target),
                device_id_type=MESH,
            )
        )
    for copy in copies[2:]:
        copy.start()
    pl.when(lat < lat_size - 1)(copies[0].start)
    pl.when(lat > 0)(copies[1].start)

    upper_core, lower_core = core == cores - 1, core == 0

    def tell(sem, targets):
        for target in targets:
            pl.semaphore_signal(sem, inc=1, device_id=(lat, target), device_id_type=MESH)

    def ascend():
        tell(up_sem, [above, east] if cores > 1 else [above])

    def descend():
        tell(down_sem, [below, west] if cores > 1 else [below])

    if depth > 1:
        pl.when(jnp.logical_and(first_z, upper_core))(ascend)
        pl.when(jnp.logical_and(last_z, lower_core))(descend)

    nlat = lat_size * cells
    step = 2.0 * math.pi / (lon_size * width)
    row_index = lat * cells - 1 + iota((2 * SUBS, LANES), 0)
    cosines = jnp.cos((row_index.astype(jnp.float32) + 0.5 - nlat / 2) * step)
    weights = jnp.where((row_index >= 0) & (row_index < nlat), cosines, 0.0)
    scales = 0.5 / jnp.sqrt(cosines)

    def weight(i):
        return weights[i + 1 : i + 2, :]

    def scale(i):
        return scales[i + 1 : i + 2, :]

    wide = iota((snaps, LANES), 1)

    def lon_inner(tile):
        right = jnp.where(wide == LANES - 1, 0.0, pltpu.roll(tile, LANES - 1, 1))
        return right - jnp.where(wide == 0, 0.0, pltpu.roll(tile, 1, 1))

    def lat_inner(f, i):
        high = weight(i + 1) * winds[f][i + 1] if i + 1 < cells else 0.0
        low = weight(i - 1) * winds[f][i - 1] if i > 0 else 0.0
        return high - low

    def inner(f, i):
        if f == 0:
            return lon_inner(winds[1][i]) - lat_inner(0, i)
        return lon_inner(winds[0][i]) + lat_inner(1, i)

    sides = sorted({0, cells - 1})
    middle = [i for i in range(cells) if i not in sides]
    inside = (wide > 0) & (wide < LANES - 1)
    rows_of = 2 * 2 * cells

    def take_ends(tile, f, i, held):
        at = f * cells + i
        out = []
        for t in range(parts):
            moved = roll(tile[t * SUBS : (t + 1) * SUBS], 2 * at + 1)
            out.append(held[t] + jnp.where(lane // 2 == at, moved, 0.0))
        return out

    held = [jnp.zeros((SUBS, LANES), jnp.float32)] * parts
    tiles = []
    for f in range(2):
        for i in middle:
            tile = inner(f, i) * scale(i)
            x_ref[f * cells + i] = tile
            held = take_ends(tile, f, i, held)
            tiles.append(jnp.where(inside, tile, 0.0))
        for i in sides:
            x_ref[f * cells + i] = inner(f, i)
    for t in range(parts):
        ends_ref[t] = held[t]
    if middle:
        high, low = gram_pair(tiles, snaps)
        inner_ref[0] = high
        inner_ref[1] = low

    if depth > 1:
        @pl.when(jnp.logical_not(first_z))
        def _():
            pl.semaphore_wait(up_sem, 1)
            pl.when(jnp.logical_and(upper_core, jnp.logical_not(last_z)))(ascend)

        @pl.when(jnp.logical_not(last_z))
        def _():
            pl.semaphore_wait(down_sem, 1)
            pl.when(jnp.logical_and(lower_core, jnp.logical_not(first_z)))(descend)

    for at, copy in enumerate(copies):
        if at == 0:
            pl.when(lat > 0)(copy.wait_recv)
        elif at == 1:
            pl.when(lat < lat_size - 1)(copy.wait_recv)
        else:
            copy.wait_recv()

    across = jnp.zeros((SUBS, LANES), jnp.float32)
    for i in range(cells):
        across = jnp.where(lane // 2 % cells == i, scale(i), across)
    across = jnp.where(lane < rows_of, across, 0.0)
    ends = []
    for t in range(parts):
        from_east = roll(lon_in[1], -1 - t * rows_of)
        from_west = roll(lon_in[0], 1 - t * rows_of)
        ends.append(jnp.where(lane % 2 == 0, from_east, -from_west) * across)

    held = [ends_ref[t] for t in range(parts)]
    tiles = []
    for f in range(2):
        for i in sides:
            edge = 0.0
            if i == cells - 1:
                edge = edge + weight(cells) * lat_in[1, f]
            if i == 0:
                edge = edge - weight(-1) * lat_in[0, f]
            tile = x_ref[f * cells + i]
            tile = (tile - edge if f == 0 else tile + edge) * scale(i)
            x_ref[f * cells + i] = tile
            held = take_ends(tile, f, i, held)
            tiles.append(jnp.where(inside, tile, 0.0))
    tiles.append(jnp.concatenate([held[t] + ends[t] for t in range(parts)], axis=0))
    high, low = gram_pair(tiles, snaps)
    if middle:
        high, more = two_sum(high, inner_ref[0])
        high, low = two_sum(high, low + (more + inner_ref[1]))

    def whole_tile(f, i):
        at = f * cells + i
        tile = x_ref[at]
        edge = jnp.concatenate([roll(ends[t], -2 * at - 1) for t in range(parts)], axis=0)
        return jnp.where(inside, tile, tile + edge)

    pending = []

    def exchange(buf, slot, count, target, at, parts):
        rows = 0
        for part in parts:
            buf[slot, pl.ds(rows, part.shape[0])] = part
            rows += part.shape[0]
        for d in peer_order(count):
            copy = pltpu.make_async_remote_copy(
                src_ref=buf.at[slot],
                dst_ref=buf.at[slot],
                send_sem=sum_send.at[at],
                recv_sem=sum_recv.at[at],
                device_id=target(shifted(slot, d, count)),
                device_id_type=pl.DeviceIdType.LOGICAL,
            )
            copy.start()
        if at == 0:
            for f in range(2):
                for i in range(cells):
                    column = (f * cells + i) * width
                    for index, part in enumerate(three(whole_tile(f, i))):
                        x_parts[pl.ds(index * snaps, snaps), pl.ds(column, width)] = part
        arrived = buf.at[pl.ds(0, count - 1)]
        pending.append((arrived, sum_send.at[at]))
        pltpu.make_async_copy(arrived, arrived, sum_recv.at[at]).wait()
        edges = [buf[index, pl.ds(SUBS, 1)] for index in range(count)]
        while len(edges) > 1:
            edges = [sum(edges[at : at + 2]) for at in range(0, len(edges), 2)]
        zero = jnp.zeros((SUBS, LANES), jnp.float32)
        totals = []
        for index in range(count):
            error = buf[index, pl.ds(SUBS + 1, SUBS)] if len(parts) > 2 else zero
            totals.append((buf[index, pl.ds(0, SUBS)], error))
        while len(totals) > 1:
            merged = []
            for at in range(0, len(totals) - 1, 2):
                (a, b), (x, y) = totals[at], totals[at + 1]
                high, low = two_sum(a, x)
                merged.append((high, low + (b + y)))
            if len(totals) % 2:
                merged.append(totals[-1])
            totals = merged
        return totals[0][0], edges[0], totals[0][1]

    bundle = message(high, low, snaps)
    if len(sum_bufs) == 1:
        everyone = lat_size * lon_size
        bundle = exchange(sum_bufs[0], lat * lon_size + lon, everyone, lambda at: at, 0, bundle)
    else:
        bundle = exchange(sum_bufs[0], lon, lon_size, lambda at: lat * lon_size + at, 0, bundle)
        bundle = exchange(sum_bufs[1], lat, lat_size, lambda at: at * lon_size + lon, 1, bundle)
    local, edge, error = bundle
    ahead = place(snaps)
    total, error = two_sum(local, error)
    total = jnp.where(ahead > 0, total + error, total)
    error = jnp.where(ahead > 0, 0.0, error)

    groups = snaps // SUBS
    sub = iota((SUBS, LANES), 0)
    high, low = restore(total, error, edge, snaps)
    first, lower = factorize(
        lambda g, k: total[:, g * snaps + k : g * snaps + k + 1],
        [high[g * SUBS : (g + 1) * SUBS] for g in range(groups)],
        snaps,
        snaps,
    )
    inverse = first[:, :snaps]
    hold_ref[0] = first
    gap = residual(high, low, lower, snaps)
    moved = pair_dot(gap, inverse, ((1,), (1,)))
    moved = pair_dot(inverse, moved, ((1,), (0,)))
    start = []
    for g in range(groups):
        at = iota((SUBS, snaps), 0) + g * SUBS
        unit = jnp.where(iota((SUBS, snaps), 1) == at, 1.0, 0.0)
        start.append(moved[g * SUBS : (g + 1) * SUBS] + unit)
    hold_ref[1, :, :snaps] = moved

    for at, copy in enumerate(copies):
        if at == 0:
            pl.when(lat < lat_size - 1)(copy.wait_send)
        elif at == 1:
            pl.when(lat > 0)(copy.wait_send)
        else:
            copy.wait_send()
    for sent, send in pending:
        pltpu.make_async_copy(sent, sent, send).wait()

    w = [part.astype(jnp.float32) for part in three(hold_ref[0])]
    quarters = LANES // snaps
    terms = [(0, 0), (0, 1), (0, 2), (1, 0), (1, 1), (2, 0)]
    left = []
    for at in range(0, len(terms), quarters):
        tiles = [
            pltpu.roll(w[a], index * snaps, 1) if index else w[a]
            for index, (a, b) in enumerate(terms[at : at + quarters])
        ]
        left.append(sum(tiles[1:], tiles[0]).astype(jnp.bfloat16))
    left = jnp.concatenate(left, axis=1)[:, : len(terms) * snaps]
    for at in range(0, 2 * cells * width, 2 * width):
        x = [x_parts[b * snaps : (b + 1) * snaps, at : at + 2 * width] for b in range(3)]
        right = jnp.concatenate([x[b] for a, b in terms], axis=0)
        solved_ref[:, at : at + 2 * width] = lax.dot_general(
            left, right, (((1,), (0,)), ((), ())), preferred_element_type=jnp.float32
        )
    second, lower_two = factorize(lambda g, k: start[g][:, k : k + 1], start, snaps, 0)
    turn_ref[...] = second * root
    factor_ref[0] = lower
    factor_ref[1] = lower_two


def shifted(me, d, count):
    if count & (count - 1) == 0:
        return me ^ d
    return (me + d) % count


def peer_order(count):
    return sorted(range(1, count), key=lambda d: (-((d >> 1) & 3), -(d >> 3), d))


def finish(root, solved_ref, turn_ref, lower_ref, modes_hbm, factor_hbm, modes_ref, flat_ref, sem):
    snaps, _, cells, width = modes_hbm.shape
    bulk, rest = two(turn_ref[...][:, :snaps])
    lower, lower_two = lower_ref[0][:, : 2 * snaps], lower_ref[1][:, :snaps]
    wide = jnp.concatenate([jnp.zeros_like(lower_two), lower_two], axis=0)
    wide = jnp.concatenate([wide, jnp.zeros((2 * snaps, LANES - snaps), jnp.float32)], axis=1)
    flat = dot(lower, wide, ((1,), (0,))) / root
    flat = jnp.transpose(flat)[:snaps, :snaps]
    stores = []

    def one(m, n):
        return lax.dot_general(
            m, n, (((1,), (0,)), ((), ())), preferred_element_type=jnp.float32
        )

    for f in range(2):
        for i in range(0, cells, 2):
            at = (f * cells + i) * width
            main, tail = two(solved_ref[:, at : at + 2 * width])
            modes = one(bulk, main) + (one(bulk, tail) + one(rest, main))
            for c in range(2):
                modes_ref[f, i + c] = modes[:, c * width : (c + 1) * width]
                stores.append(
                    pltpu.make_async_copy(modes_ref.at[f, i + c], modes_hbm.at[:, f, i + c], sem)
                )
                stores[-1].start()
    flat_ref[...] = flat
    stores.append(pltpu.make_async_copy(flat_ref, factor_hbm, sem))
    stores[-1].start()
    for store in stores:
        store.wait()


def shards(sizes, wind_u, wind_v):
    snaps, cells, width = wind_u.shape
    lat_size, lon_size, cores = sizes
    chips = lat_size * lon_size // cores
    f32 = jnp.float32
    dma = pltpu.SemaphoreType.DMA
    vmem = pl.BlockSpec(memory_space=pltpu.VMEM)
    hbm = pl.BlockSpec(memory_space=pltpu.HBM)
    root = math.sqrt(2 * lat_size * cells * lon_size * width)
    if lat_size * lon_size <= DIRECT:
        sum_bufs = [pltpu.VMEM((lat_size * lon_size, SUBS + 1, LANES), f32)]
    else:
        sum_bufs = [
            pltpu.VMEM((lon_size, SUBS + 1, LANES), f32),
            pltpu.VMEM((lat_size, 2 * SUBS + 1, LANES), f32),
        ]
    held = pl.pallas_call(
        functools.partial(kernel, sizes, root),
        out_shape=(
            pltpu.VMEM((snaps, 2 * cells * width), f32),
            pltpu.VMEM((snaps, LANES), f32),
            pltpu.VMEM((2, snaps, LANES), f32),
        ),
        in_specs=[hbm, hbm],
        out_specs=(vmem, vmem, vmem),
        scratch_shapes=[
            pltpu.VMEM((2, cells, snaps, width), f32),
            pltpu.VMEM((2 * cells, snaps, width), f32),
            pltpu.VMEM((2, snaps, LANES), f32),
            pltpu.VMEM((snaps // SUBS, SUBS, LANES), f32),
            pltpu.VMEM((2, SUBS, LANES), f32),
            pltpu.VMEM((2, 2, snaps, width), f32),
            pltpu.VMEM((SUBS, LANES), f32),
            pltpu.VMEM((2, SUBS, LANES), f32),
            pltpu.VMEM((3 * snaps, 2 * cells * width), jnp.bfloat16),
            sum_bufs,
            dma((2,)),
            dma((2,)),
            dma((2,)),
            dma((2,)),
            dma((len(sum_bufs),)),
            dma((len(sum_bufs),)),
            pltpu.SemaphoreType.REGULAR,
            pltpu.SemaphoreType.REGULAR,
            dma,
        ],
        compiler_params=pltpu.CompilerParams(
            collective_id=0, has_side_effects=True, vmem_limit_bytes=VMEM_BYTES
        ),
    )(*(pltpu.with_memory_space_constraint(w, pltpu.HBM) for w in (wind_u, wind_v)))
    anywhere = pl.BlockSpec(memory_space=pl.ANY)
    return pl.pallas_call(
        functools.partial(finish, root),
        out_shape=(
            jax.ShapeDtypeStruct((snaps, 2, cells, width), f32),
            jax.ShapeDtypeStruct((snaps, snaps), f32),
        ),
        in_specs=[vmem, vmem, vmem],
        out_specs=(anywhere, anywhere),
        scratch_shapes=[
            pltpu.VMEM((2, cells, snaps, width), f32),
            pltpu.VMEM((snaps, snaps), f32),
            dma,
        ],
        compiler_params=pltpu.CompilerParams(vmem_limit_bytes=VMEM_BYTES),
    )(*held)


def solution(mesh):
    lat_size, lon_size = mesh.shape["lat"], mesh.shape["lon"]
    sizes = (lat_size, lon_size, 2 if lon_size % 2 == 0 else 1)
    in_specs = (P(None, "lat", "lon"), P(None, "lat", "lon"))
    out_specs = (P(None, None, "lat", "lon"), P())
    return jax.shard_map(
        functools.partial(shards, sizes),
        mesh=mesh,
        in_specs=in_specs,
        out_specs=out_specs,
        check_vma=False,
    )
```
